32 devices in a mesh: rows: 8 (over y, x, core), chan: 4 (over z).
Axes of the slice: x: 2, y: 2, z: 4, core: 2. Of those that a mesh axis runs over, the one named last changes fastest.
Arguments:
- latents: bfloat16 [512, 4, 8, 128], P('chan', None, 'rows'), may hold values from -20 to 20
- cache_one: bfloat16 [512, 2, 8, 128], P('chan', None, 'rows'), may hold values from -4 to 4
- cache_two: bfloat16 [512, 2, 8, 128], P('chan', None, 'rows'), may hold values from -4 to 4
- gain_one: float32 [512], P('chan'), may hold values from 0.25 to 1.75
- bias_one: float32 [512], P('chan'), may hold values from -0.8 to 0.8
- weight_one: bfloat16 [3, 3, 3, 512, 512], P(None, None, None, None, 'chan'), may hold values from -0.0546875 to 0.0546875
- gain_two: float32 [512], P('chan'), may hold values from 0.25 to 1.75
- bias_two: float32 [512], P('chan'), may hold values from -0.8 to 0.8
- weight_two: bfloat16 [3, 3, 3, 512, 512], P(None, None, None, 'chan'), may hold values from -0.0625 to 0.0625
Outputs:
- upsampled: float32 [512, 4, 16, 256], P('chan', None, 'rows')
The draws below stay inside these ranges and needn't reach their ends.
All inputs are finite; a program needn't handle non-finite values.
Results may differ from the reference program's by a relative error of at most 0.0022.
Values may be sent and summed in bfloat16 or wider, within the bound.
A program may use at most 64 MiB of HBM per device.

```python
import jax
import jax.numpy as jnp
from jax import lax

CHANNELS = 512
GROUPS = 32
FRAMES = 4
WIDTH = 128
HEIGHT = 8


def draw_latents(key, part):
    folded = jax.random.fold_in(key, 7)
    jitter_key, chan_key = jax.random.split(folded, 2)
    extent = (CHANNELS, FRAMES, HEIGHT, WIDTH)
    heights = jnp.arange(HEIGHT, dtype=jnp.float32) / (HEIGHT - 1)
    chan_scale = jnp.exp(jax.random.uniform(chan_key, (CHANNELS,), jnp.float32, -0.69, 0.69))
    jitter = jnp.clip(jax.random.normal(jitter_key, extent, jnp.float32), -3.0, 3.0)
    row_scale = 0.3 * 10.0 ** heights
    return (jitter * row_scale[None, None, :, None] * chan_scale[:, None, None, None]).astype(jnp.bfloat16)


def strengthened(drawn, rng, source, target, shards_of, factor):
    def block_of(axis_at):
        return (jnp.arange(drawn.shape[axis_at]) // (drawn.shape[axis_at] // shards_of)).reshape((-1,) + (1,) * (drawn.ndim - 1 - axis_at))

    near = jax.random.permutation(rng, shards_of)[block_of(target)]
    other_side = (block_of(target) + shards_of // 2) % shards_of
    return jnp.where((block_of(source) == near) | (block_of(source) == other_side), factor * drawn, drawn)


def block_scale(own_key, dims, pieces, least, top_value):
    def one(dim, shards_of):
        steps = jax.random.uniform(jax.random.fold_in(jax.random.fold_in(own_key, 6), dim), (shards_of,), jnp.float32, least / len(pieces), top_value / len(pieces))
        return jnp.repeat(jnp.exp(steps), dims[dim] // shards_of).reshape((-1,) + (1,) * (len(dims) - dim - 1))

    loudness = one(*pieces[0])
    for cut in pieces[1:]:
        loudness = loudness * one(*cut)
    return loudness


def scatter_about(rng, dims, deviation, bound, shards=(), held_as=jnp.bfloat16):
    array = deviation * jax.random.normal(rng, dims, jnp.float32)
    if shards:
        array = array * block_scale(rng, dims, shards, -0.22, 0.18)
    return jnp.clip(array, -bound, bound).astype(held_as)


def heavy_noise(rng, shape, scale, limit, pieces, heavy, kind=jnp.bfloat16):
    values = scale * jax.random.normal(rng, shape, jnp.float32)
    if pieces:
        values = values * block_scale(rng, shape, pieces, -0.22, 0.18)
    return jnp.clip(strengthened(values, jax.random.fold_in(rng, 3), *heavy), -limit, limit).astype(kind)


def setup_inputs(seed: int = 0) -> dict:
    seeds = jax.random.split(jax.random.key(seed), 10)
    return {
        "latents": draw_latents(jax.random.fold_in(seeds[9], 71), 0),
        "cache_one": scatter_about(seeds[1], (CHANNELS, 2, HEIGHT, WIDTH), 1.0, 4.0, ((0, 4), (2, 8))),
        "cache_two": scatter_about(seeds[2], (CHANNELS, 2, HEIGHT, WIDTH), 1.0, 4.0, ((0, 4), (2, 8))),
        "gain_one": jnp.clip(1.0 + 0.15 * jax.random.normal(seeds[3], (CHANNELS,), jnp.float32), 0.25, 1.75),
        "bias_one": jnp.clip(jax.random.uniform(seeds[4], (CHANNELS,), jnp.float32, -0.8, 0.8) * block_scale(seeds[4], (CHANNELS,), ((0, 4),), -0.4, 0.0), -0.8, 0.8),
        "weight_one": scatter_about(seeds[5], (3, 3, 3, CHANNELS, CHANNELS), (27 * CHANNELS) ** -0.5, 0.0546875, ((4, 4),)),
        "gain_two": jnp.clip(1.0 + 0.15 * jax.random.normal(seeds[6], (CHANNELS,), jnp.float32), 0.25, 1.75),
        "bias_two": jnp.clip(jax.random.uniform(seeds[7], (CHANNELS,), jnp.float32, -0.8, 0.8) * block_scale(seeds[7], (CHANNELS,), ((0, 4),), -0.4, 0.0), -0.8, 0.8),
        "weight_two": heavy_noise(seeds[8], (3, 3, 3, CHANNELS, CHANNELS), (27 * CHANNELS) ** -0.5, 0.0625, ((3, 4),), (3, 4, 4, 2.0)),
    }


epsilon = 1e-06

def group_silu(values, gain, bias):
    grouped = values.reshape(GROUPS, CHANNELS // GROUPS, FRAMES, HEIGHT, WIDTH)
    average = lax.optimization_barrier(jnp.mean(grouped, axis=(1, 2, 3, 4), keepdims=True))
    spread = lax.optimization_barrier(jnp.mean((grouped - average) ** 2, axis=(1, 2, 3, 4), keepdims=True))
    normed = ((grouped - average) * lax.rsqrt(spread + epsilon)).reshape(CHANNELS, FRAMES, HEIGHT, WIDTH)
    scaled = normed * gain[:, None, None, None] + bias[:, None, None, None]
    return jax.nn.silu(scaled).astype(jnp.bfloat16)

def convolve(cache, field, kernel):
    frames = jnp.concatenate([cache, field], axis=1).astype(jnp.float32)
    result = lax.conv_general_dilated(frames[None], kernel.astype(jnp.float32), (1, 1, 1), ((0, 0), (1, 1), (1, 1)), dimension_numbers=('NCDHW', 'DHWIO', 'NCDHW'), precision=lax.Precision.HIGHEST)
    return result[0]

def reference(latents, cache_one, cache_two, gain_one, bias_one, weight_one, gain_two, bias_two, weight_two):
    floats = latents.astype(jnp.float32)
    first = group_silu(floats, gain_one, bias_one)
    middle = convolve(cache_one, first, weight_one).astype(jnp.bfloat16)
    second = group_silu(middle.astype(jnp.float32), gain_two, bias_two)
    result = floats + convolve(cache_two, second, weight_two)
    return jnp.repeat(jnp.repeat(result, 2, axis=2), 2, axis=3)
```

```python
import functools

import jax
import jax.numpy as jnp
from jax import lax
from jax.experimental import pallas as pl
from jax.experimental.pallas import tpu as pltpu
from jax.sharding import PartitionSpec as P

CHANNELS = 512
GROUPS = 32
MESH = pl.DeviceIdType.MESH
OUT = pl.ANY
F32 = jnp.float32
BF16 = jnp.bfloat16


epsilon = 1e-06


def padded(block, sides, width):
    for axis, dim in sides:
        count = lax.axis_size(axis)
        forward = [(i, i + 1) for i in range(count - 1)]
        backward = [(target, source) for source, target in forward]
        low = lax.ppermute(
            lax.slice_in_dim(block, block.shape[dim] - width, None, axis=dim), axis, forward
        )
        high = lax.ppermute(lax.slice_in_dim(block, 0, width, axis=dim), axis, backward)
        block = jnp.concatenate([low, block, high], axis=dim)
    return block


def group_silu(values, gain, bias):
    group_size = CHANNELS // GROUPS
    grouped = values.reshape(values.shape[0] // group_size, -1)
    sums, squares = lax.psum((jnp.sum(grouped, axis=1), jnp.sum(grouped * grouped, axis=1)), "rows")
    members = grouped.shape[1] * lax.axis_size("rows")
    average = sums / members
    spread = squares / members - average * average
    normed = ((grouped - average[:, None]) * lax.rsqrt(spread + epsilon)[:, None]).reshape(
        values.shape
    )
    scaled = normed * gain[:, None, None, None] + bias[:, None, None, None]
    return jax.nn.silu(scaled).astype(jnp.bfloat16)


def pad_rows(frames):
    return padded(frames, (("rows", 2),), 1)


def conv_block(frames, kernel):
    result = lax.conv_general_dilated(
        frames[None],
        kernel,
        (1, 1, 1),
        ((0, 0), (0, 0), (1, 1)),
        dimension_numbers=("NCDHW", "DHWIO", "NCDHW"),
        preferred_element_type=jnp.float32,
    )
    return result[0]


def gathered_conv(frames, kernel):
    channels = lax.all_gather(frames, "chan", axis=0, tiled=True)
    return conv_block(channels, kernel)


def plain_body(
    latents, cache_one, cache_two, gain_one, bias_one, weight_one, gain_two, bias_two, weight_two
):
    floats = latents.astype(jnp.float32)
    first = group_silu(floats, gain_one, bias_one)
    frames_one = pad_rows(jnp.concatenate([cache_one, first], axis=1))
    middle = gathered_conv(frames_one, weight_one).astype(jnp.bfloat16)
    second = group_silu(middle.astype(jnp.float32), gain_two, bias_two)
    frames_two = pad_rows(jnp.concatenate([cache_two, second], axis=1))
    columns = lax.all_to_all(weight_two, "chan", split_axis=4, concat_axis=3, tiled=True)
    result = floats + gathered_conv(frames_two, columns)
    return jnp.repeat(jnp.repeat(result, 2, axis=2), 2, axis=3)


def block_kernel(
    R, Z, CL, T, W,
    lat_hbm, c1_hbm, c2_hbm, g1_hbm, b1_hbm, g2_hbm, b2_hbm, w1_hbm, w2_hbm,
    out_ref,
    lat_v, c1_v, c2_v, g1, b1, g2, b2,
    tmp, lat_t, raw, xc, xs1, xsc, acc1, part_out, part_in, mid, mid_in, x2, xs2, acc2,
    st1, st2, coef, rs_out, rs_in, w1, w2, out_v,
    isem, wsem, ls, lr, cs, cr, ks, kr, hs, hr, s1s, s1r, ps, pr, ms, mr, s2s, s2r, rss, rsr, osem,
):
    row = lax.axis_index("rows")
    me = lax.axis_index("chan")
    M = T * W
    C2 = 2 * W
    H = M // 2
    HL = CL * T // 2
    OWN = Z - 1
    has_up = row > 0
    has_down = row < R - 1
    edge = jnp.logical_or(me == 0, me == Z - 1)
    inner = jnp.logical_not(edge)
    is_inner = ((me + 1) // 2) % 2

    def partner(k):
        other = me * 0
        bit = 1
        while bit < Z:
            mine = (me // bit) % 2
            other = other + bit * ((1 - mine) if k & bit else mine)
            bit *= 2
        return other

    barrier = pltpu.get_barrier_semaphore()
    for k in range(1, R):
        pl.semaphore_signal(barrier, inc=1, device_id={"rows": lax.rem(row + k, R)}, device_id_type=MESH)
    for k in range(1, Z):
        pl.semaphore_signal(barrier, inc=1, device_id={"chan": partner(k)}, device_id_type=MESH)

    loads = [
        pltpu.make_async_copy(src, dst, isem.at[i])
        for i, (src, dst) in enumerate(
            [
                (lat_hbm, lat_v), (c1_hbm, c1_v), (c2_hbm, c2_v),
                (g1_hbm, g1), (b1_hbm, b1), (g2_hbm, g2), (b2_hbm, b2),
            ]
        )
    ]
    place = (0, 2, 1)
    w_copies = []
    for dt in range(3):
        for dh in range(3):
            w_copies.append(
                pltpu.make_async_copy(
                    w1_hbm.at[dt, dh],
                    w1.at[dt, :, :, pl.ds(place[dh] * CL, CL)],
                    wsem.at[dt * 3 + dh],
                )
            )
    w2_copy = pltpu.make_async_copy(w2_hbm, w2, wsem.at[9])
    for copy in loads:
        copy.start()

    def to_chan(src, dst, send, recv, k):
        return pltpu.make_async_remote_copy(
            src_ref=src, dst_ref=dst, send_sem=send, recv_sem=recv,
            device_id={"chan": partner(k)}, device_id_type=MESH,
        )

    def to_row(src, dst, send, recv, k):
        return pltpu.make_async_remote_copy(
            src_ref=src, dst_ref=dst, send_sem=send, recv_sem=recv,
            device_id={"rows": lax.rem(row + k, R)}, device_id_type=MESH,
        )

    def along(src, buffer, send, recv, d, part, side):
        slot = OWN - side * d
        return pltpu.make_async_remote_copy(
            src_ref=src, dst_ref=buffer.at[(slot - side, *part)],
            send_sem=send, recv_sem=recv,
            device_id={"chan": me + side}, device_id_type=MESH,
        )

    def latent_hop(d, ch, side):
        slot = OWN - side * d
        rows = pl.ds(ch * HL, HL)
        src = lat_hbm.at[rows] if d == 0 else raw.at[slot, rows]
        return along(
            src, raw, ls.at[(side + 1) // 2, d, ch], lr.at[slot - side, ch], d, (rows,), side
        )

    def cache_hop(d, side):
        slot = OWN - side * d
        return along(
            xc.at[slot], xc, cs.at[(side + 1) // 2, d], cr.at[slot - side], d, (), side
        )

    def arrives(d, side):
        return me >= d if side > 0 else me + d <= Z - 1

    def goes(d, side):
        return jnp.logical_and(arrives(d, side), me < Z - 1 if side > 0 else me > 0)

    def pass_on(hop, d):
        for side in (1, -1):
            if d > 0:

                @pl.when(arrives(d, side))
                def _():
                    hop(d - 1, side).wait_recv()

            if d < Z - 1:

                @pl.when(goes(d, side))
                def _():
                    hop(d, side).start()

    def latent_part(ch):
        return lambda d, side: latent_hop(d, ch, side)

    members = F32(R * M * (CHANNELS // GROUPS))
    gi = lax.broadcasted_iota(jnp.int32, (CL, CL), 0) // (CHANNELS // GROUPS)
    gj = lax.broadcasted_iota(jnp.int32, (CL, CL), 1) // (CHANNELS // GROUPS)
    same_group = (gi == gj).astype(F32)
    which = lax.broadcasted_iota(jnp.int32, (8, CL), 0)

    def local_stats(values):
        sums = jnp.sum(values, axis=0, keepdims=True)
        squares = jnp.sum(values * values, axis=0, keepdims=True)
        return jnp.where(which == 0, sums, jnp.where(which == 1, squares, 0.0))

    def share_stats(st, send, recv):
        copies = [to_row(st.at[0], st.at[k], send.at[k], recv.at[k], k) for k in range(1, R)]
        for copy in copies:
            copy.start()
        return copies

    def finish_stats(copies, st, g_ref):
        for copy in copies:
            copy.wait_recv()
        total = st[0]
        for k in range(1, R):
            total = total + st[k]
        total = jnp.dot(
            total, same_group, preferred_element_type=F32, precision=lax.Precision.HIGHEST
        ) / members
        mean = total[0:1, :]
        spread = jnp.maximum(total[1:2, :] - mean * mean, 0.0)
        return mean, lax.rsqrt(spread + epsilon) * g_ref[...]

    def normed(values, coefs):
        mean, scale, bias = coefs
        u = (values - mean) * scale + bias
        return (u / (1.0 + jnp.exp(-u))).astype(BF16)

    def shifted(block):
        rows = block.shape[0]
        cell = lax.broadcasted_iota(jnp.int32, (rows, CL), 0) % W
        wide = block.astype(F32)
        left = jnp.where(cell == 0, 0.0, pltpu.roll(wide, 1, 0)).astype(BF16)
        right = jnp.where(cell == W - 1, 0.0, pltpu.roll(wide, rows - 1, 0)).astype(BF16)
        return left, block, right

    def put(dst, rows, column, block):
        for dx, value in enumerate(shifted(block)):
            dst[rows, column + dx * CL : column + (dx + 1) * CL] = value

    with jax.named_scope("barrier wait"):
        pl.semaphore_wait(barrier, R - 1 + Z - 1)

    for ch in range(2):
        pass_on(latent_part(ch), 0)
    for copy in w_copies:
        copy.start()

    with jax.named_scope("own latents"):
        loads[0].wait()
        tmp[...] = lat_v[...].astype(F32)
        for t in range(T):
            lat_t[t * W : (t + 1) * W, :] = tmp[pl.ds(t, CL, stride=T), :].T
        st1[0] = local_stats(lat_t[...])
        stats_one = share_stats(st1, s1s, s1r)

    with jax.named_scope("own caches"):
        loads[1].wait()
        tmp[0 : 2 * CL, :] = c1_v[...].astype(F32)
        for t in range(2):
            xc[OWN, t * W : (t + 1) * W, :] = tmp[pl.ds(t, CL, stride=2), :].T.astype(BF16)
        loads[2].wait()
        tmp[0 : 2 * CL, :] = c2_v[...].astype(F32)
        for t in range(2):
            x2[1, t * W : (t + 1) * W, :] = tmp[pl.ds(t, CL, stride=2), :].T.astype(BF16)
        acc1[...] = jnp.zeros_like(acc1)

    halo_down = to_row(x2.at[1], x2.at[0], hs.at[0], hr.at[0], 1)
    halo_up = to_row(x2.at[1], x2.at[2], hs.at[1], hr.at[1], R - 1)

    def kernel_one(dt, z, low, high):
        base = pl.ds(pl.multiple_of(z * CL, CL), CL)
        return jnp.concatenate([w1[dt, dx, base, low:high] for dx in range(3)], axis=0)

    def latent_dots(z):
        for dt in (2, 1, 0):
            start = (2 - dt) * W
            acc1[start:, :] += jnp.dot(
                xs1[0 : M - start, :], kernel_one(dt, z, 0, 3 * CL), preferred_element_type=F32
            )

    def cache_dots(z, low, high):
        for dt in range(2):
            acc1[0 : C2 - dt * W, low:high] += jnp.dot(
                xsc[dt * W : C2, :], kernel_one(dt, z, low, high), preferred_element_type=F32
            )

    def place_caches(slot):
        for t in range(2):
            rows = slice(t * W, (t + 1) * W)
            put(xsc, rows, 0, xc[slot, rows, :])

    def place_latents(slot, coefs):
        tmp[...] = raw[slot].astype(F32)
        for t in range(T):
            put(
                xs1, slice(t * W, (t + 1) * W), 0,
                normed(tmp[pl.ds(t, CL, stride=T), :].T, coefs),
            )

    for copy in w_copies:
        copy.wait()
    w2_copy.start()
    with jax.named_scope("own cache dots"):
        place_caches(OWN)
        cache_dots(me, 0, 3 * CL)
    pass_on(cache_hop, 0)
    with jax.named_scope("stats one"):
        for copy in loads[3:]:
            copy.wait()
        mean, scale = finish_stats(stats_one, st1, g1)
        bias = b1[...]
        coef[0] = jnp.where(which == 0, mean, jnp.where(which == 1, scale, bias))
        coef_copies = [
            to_chan(coef.at[0], coef.at[k], ks.at[k], kr.at[k], k) for k in range(1, Z)
        ]
        for copy in coef_copies:
            copy.start()

    @pl.when(has_down)
    def _():
        halo_down.start()

    @pl.when(has_up)
    def _():
        halo_up.start()

    with jax.named_scope("latents 1"):
        for ch in range(2):
            pass_on(latent_part(ch), 1)
    with jax.named_scope("own latent dots"):
        for t in range(T):
            rows = slice(t * W, (t + 1) * W)
            put(xs1, rows, 0, normed(lat_t[rows, :], (mean, scale, bias)))
        latent_dots(me)

    with jax.named_scope("latents 2"):
        for ch in range(2):
            pass_on(latent_part(ch), 2)

    def plane(k):
        if k == 1:
            return partner(1), 1
        a, b = partner(2), partner(3)
        if k == 2:
            return a + is_inner * (b - a), 2 + is_inner
        return b + is_inner * (a - b), 3 - is_inner

    def other_latents(k):
        z, at = plane(k)
        place_latents(OWN + z - me, tuple(coef[at, i : i + 1, :] for i in range(3)))
        latent_dots(z)

    with jax.named_scope("coef wait 1"):
        coef_copies[0].wait_recv()
    with jax.named_scope("latent dots 1"):
        other_latents(1)
    with jax.named_scope("caches 1"):
        pass_on(cache_hop, 1)
    with jax.named_scope("coef wait 2"):
        coef_copies[1].wait_recv()
        coef_copies[2].wait_recv()
    with jax.named_scope("latent dots 2"):
        other_latents(2)
    with jax.named_scope("latents 3"):
        for ch in range(2):
            pass_on(latent_part(ch), 3)
    with jax.named_scope("latent dots 3"):
        other_latents(3)

    def rows_of(half):
        return slice(half * H, (half + 1) * H)

    def part_copies(half):
        rows = rows_of(half)
        return (
            to_row(part_out.at[0, rows], part_in.at[0, rows], ps.at[0, half], pr.at[0, half], 1),
            to_row(part_out.at[1, rows], part_in.at[1, rows], ps.at[1, half], pr.at[1, half], R - 1),
        )

    def mid_copies(half):
        rows = rows_of(half)
        return (
            to_row(mid.at[rows], mid_in.at[0, rows], ms.at[0, half], mr.at[0, half], 1),
            to_row(mid.at[rows], mid_in.at[1, rows], ms.at[1, half], mr.at[1, half], R - 1),
        )

    def start_rows(copies):
        down, up = copies

        @pl.when(has_down)
        def _():
            down.start()

        @pl.when(has_up)
        def _():
            up.start()

    def send_parts(half):
        rows = rows_of(half)
        part_out[0, rows] = acc1[rows, 0:CL].astype(BF16)
        part_out[1, rows] = acc1[rows, CL : 2 * CL].astype(BF16)
        start_rows(part_copies(half))

    def finish_mid(half):
        rows = rows_of(half)
        down, up = part_copies(half)

        @pl.when(has_up)
        def _():
            down.wait_recv()
            acc1[rows, 2 * CL :] += part_in[0, rows].astype(F32)

        @pl.when(has_down)
        def _():
            up.wait_recv()
            acc1[rows, 2 * CL :] += part_in[1, rows].astype(F32)

        mid[rows] = acc1[rows, 2 * CL :].astype(BF16)
        return local_stats(mid[rows].astype(F32))

    with jax.named_scope("parts of half 1"):
        send_parts(1)
        pass_on(cache_hop, 2)
    with jax.named_scope("cache dots 1"):
        z, _ = plane(1)
        place_caches(OWN + z - me)
        cache_dots(z, 0, 3 * CL)
    with jax.named_scope("cache dots 2"):
        z, _ = plane(2)
        place_caches(OWN + z - me)
        cache_dots(z, 0, 3 * CL)

    with jax.named_scope("conv2 of caches"):
        w2_copy.wait()

        @pl.when(has_up)
        def _():
            halo_down.wait_recv()

        @pl.when(has_down)
        def _():
            halo_up.wait_recv()

        @pl.when(jnp.logical_not(has_up))
        def _():
            x2[0] = jnp.zeros((C2, CL), BF16)
            xs2[C2:, 0 : 3 * CL] = jnp.zeros((M, 3 * CL), BF16)

        @pl.when(jnp.logical_not(has_down))
        def _():
            x2[2] = jnp.zeros((C2, CL), BF16)
            xs2[C2:, 6 * CL :] = jnp.zeros((M, 3 * CL), BF16)

        for dh in range(3):
            put(xs2, slice(0, C2), dh * 3 * CL, x2[dh])
        both = jnp.dot(xs2[0:C2, :], w2[0], preferred_element_type=F32)
        one = jnp.dot(xs2[W:C2, :], w2[1], preferred_element_type=F32)
        for d in range(Z):
            cols = slice(d * CL, (d + 1) * CL)
            acc2[d, 0:W] = both[0:W, cols] + one[:, cols]
            acc2[d, W:C2] = both[W:C2, cols]

    with jax.named_scope("mid of half 1"):
        partial = finish_mid(1)

    with jax.named_scope("caches 3"):
        pass_on(cache_hop, 3)
    with jax.named_scope("cache dots 3"):
        z, _ = plane(3)
        place_caches(OWN + z - me)
        cache_dots(z, 0, 3 * CL)
        send_parts(0)
    with jax.named_scope("mid of half 0"):
        st2[0] = partial + finish_mid(0)
        stats_two = share_stats(st2, s2s, s2r)
        start_rows(mid_copies(0))
        start_rows(mid_copies(1))
    with jax.named_scope("stats two"):
        coefs_two = (*finish_stats(stats_two, st2, g2), b2[...])

    def place_mid(half):
        rows = rows_of(half)
        there = slice(C2 + half * H, C2 + (half + 1) * H)
        put(xs2, there, 3 * CL, normed(mid[rows].astype(F32), coefs_two))
        down, up = mid_copies(half)

        @pl.when(has_up)
        def _():
            down.wait_recv()
            put(xs2, there, 0, normed(mid_in[0, rows].astype(F32), coefs_two))

        @pl.when(has_down)
        def _():
            up.wait_recv()
            put(xs2, there, 6 * CL, normed(mid_in[1, rows].astype(F32), coefs_two))

    ZH = Z // 2
    mine = me // ZH

    def second_dots(half, pair):
        cols = pl.ds(pl.multiple_of(pair * (ZH * CL), ZH * CL), ZH * CL)
        for dt in (2, 1, 0):
            first = half * H - (2 - dt) * W
            skip = max(0, -first)
            if skip >= H:
                continue
            term = jnp.dot(
                xs2[C2 + first + skip : C2 + first + H, :], w2[dt, :, cols],
                preferred_element_type=F32,
            )
            for j in range(ZH):
                rows = slice(half * H + skip, (half + 1) * H)
                cut = term[:, j * CL : (j + 1) * CL]
                if half > 0 and dt == 2:
                    acc2[pair * ZH + j, rows] = cut
                else:
                    acc2[pair * ZH + j, rows] += cut

    def sum_copy(slot, half, k, to):
        rows = rows_of(half)
        return to_chan(
            rs_out.at[k - 1, rows], rs_in.at[slot, rows], rss.at[half, k], rsr.at[half, slot], to
        )

    def send_sum(half, k, slot, to):
        rows = rows_of(half)
        rs_out[k - 1, rows] = acc2[partner(k), rows].astype(BF16)
        sum_copy(slot, half, k, to).start()

    MERGE = 0

    def send_merged(half):
        rows = rows_of(half)
        sum_copy(MERGE, half, 3, 1).wait_recv()
        rs_out[1, rows] = (acc2[partner(2), rows] + rs_in[MERGE, rows].astype(F32)).astype(BF16)
        sum_copy(2, half, 2, 2).start()

    with jax.named_scope("place half 0"):
        place_mid(0)
    with jax.named_scope("conv2 half 0 far"):
        second_dots(0, 1 - mine)

        @pl.when(edge)
        def _():
            send_sum(0, 3, MERGE, 1)

        @pl.when(inner)
        def _():
            send_sum(0, 3, 3, 3)

    with jax.named_scope("place half 1"):
        place_mid(1)
    with jax.named_scope("conv2 half 1 far"):
        second_dots(1, 1 - mine)

        @pl.when(edge)
        def _():
            send_sum(1, 3, MERGE, 1)

        @pl.when(inner)
        def _():
            send_sum(1, 3, 3, 3)

    with jax.named_scope("conv2 half 0 near"):
        second_dots(0, mine)

        @pl.when(edge)
        def _():
            send_sum(0, 2, 2, 2)

        @pl.when(inner)
        def _():
            send_sum(0, 1, 1, 1)
            send_merged(0)

    with jax.named_scope("conv2 half 1 near"):
        second_dots(1, mine)

        @pl.when(edge)
        def _():
            send_sum(1, 2, 2, 2)

        @pl.when(inner)
        def _():
            send_sum(1, 1, 1, 1)

        lat_t[...] = lat_t[...] + acc2[me]
    with jax.named_scope("last sums out"):

        @pl.when(edge)
        def _():
            sum_copy(2, 0, 2, 2).wait_send()
            send_sum(0, 1, 1, 1)
            sum_copy(2, 1, 2, 2).wait_send()
            send_sum(1, 1, 1, 1)

        @pl.when(inner)
        def _():
            send_merged(1)

    ei = lax.broadcasted_iota(jnp.int32, (W, 2 * W), 0)
    ej = lax.broadcasted_iota(jnp.int32, (W, 2 * W), 1) // 2
    twice = (ei == ej).astype(F32)

    def out_copy(half):
        return pltpu.make_async_copy(
            out_v.at[half].reshape(CL, 8, W), out_ref.at[:, half], osem.at[half]
        )

    for half in range(2):
        rows = rows_of(half)
        with jax.named_scope(f"sums wait {half}"):
            sum_copy(1, half, 1, 1).wait_recv()
            sum_copy(2, half, 2, 2).wait_recv()

            @pl.when(inner)
            def _():
                sum_copy(3, half, 3, 3).wait_recv()
                lat_t[rows, :] += rs_in[3, rows].astype(F32)

        with jax.named_scope(f"upsample {half}"):
            for t in range(half * T // 2, (half + 1) * T // 2):
                rows = slice(t * W, (t + 1) * W)
                total = lat_t[rows, :] + rs_in[1, rows].astype(F32) + rs_in[2, rows].astype(F32)
                wide = jnp.dot(
                    total.T, twice, preferred_element_type=F32, precision=lax.Precision.HIGHEST
                )
                for side in range(2):
                    for again in range(2):
                        out_v[half, pl.ds((t % 2) * 4 + side * 2 + again, CL, stride=8), :] = wide[
                            :, side * W : (side + 1) * W
                        ]
            out_copy(half).start()

    with jax.named_scope("sends wait"):
        out_copy(0).wait()
        out_copy(1).wait()
        for copy in stats_one + stats_two + coef_copies:
            copy.wait_send()
        for side in (1, -1):
            for d in range(Z - 1):

                @pl.when(goes(d, side))
                def _():
                    latent_hop(d, 0, side).wait_send()
                    latent_hop(d, 1, side).wait_send()
                    cache_hop(d, side).wait_send()

        for half in range(2):
            sum_copy(1, half, 1, 1).wait_send()
            sum_copy(1, half, 3, 1).wait_send()

            @pl.when(inner)
            def _():
                sum_copy(2, half, 2, 2).wait_send()

        @pl.when(has_down)
        def _():
            for copy in (halo_down, *(c(h)[0] for c in (part_copies, mid_copies) for h in range(2))):
                copy.wait_send()

        @pl.when(has_up)
        def _():
            for copy in (halo_up, *(c(h)[1] for c in (part_copies, mid_copies) for h in range(2))):
                copy.wait_send()


def body(
    latents, cache_one, cache_two, gain_one, bias_one, weight_one, gain_two, bias_two, weight_two
):
    CL, T, rows_here, W = latents.shape
    R, Z = lax.axis_size("rows"), lax.axis_size("chan")
    if CL != 128 or W != 128 or rows_here != 1 or T != 4 or R < 2 or Z != 4:
        return plain_body(
            latents, cache_one, cache_two, gain_one, bias_one, weight_one, gain_two, bias_two,
            weight_two,
        )
    C = CL * Z
    M = T * W
    hbm = pl.BlockSpec(memory_space=pltpu.HBM)
    dma = pltpu.SemaphoreType.DMA
    out = pl.pallas_call(
        functools.partial(block_kernel, R, Z, CL, T, W),
        out_shape=jax.ShapeDtypeStruct((CL, 2, 8, W), F32),
        in_specs=[hbm] * 9,
        out_specs=pl.BlockSpec(memory_space=OUT),
        scratch_shapes=[
            pltpu.VMEM((CL * T, W), BF16),
            pltpu.VMEM((CL * 2, W), BF16),
            pltpu.VMEM((CL * 2, W), BF16),
            pltpu.VMEM((1, CL), F32),
            pltpu.VMEM((1, CL), F32),
            pltpu.VMEM((1, CL), F32),
            pltpu.VMEM((1, CL), F32),
            pltpu.VMEM((CL * T, W), F32),
            pltpu.VMEM((M, CL), F32),
            pltpu.VMEM((2 * Z - 1, CL * T, W), BF16),
            pltpu.VMEM((2 * Z - 1, 2 * W, CL), BF16),
            pltpu.VMEM((M, 3 * CL), BF16),
            pltpu.VMEM((2 * W, 3 * CL), BF16),
            pltpu.VMEM((M, 3 * CL), F32),
            pltpu.VMEM((2, M, CL), BF16),
            pltpu.VMEM((2, M, CL), BF16),
            pltpu.VMEM((M, CL), BF16),
            pltpu.VMEM((2, M, CL), BF16),
            pltpu.VMEM((3, 2 * W, CL), BF16),
            pltpu.VMEM((M + 2 * W, 9 * CL), BF16),
            pltpu.VMEM((Z, M, CL), F32),
            pltpu.VMEM((R, 8, CL), F32),
            pltpu.VMEM((R, 8, CL), F32),
            pltpu.VMEM((Z, 8, CL), F32),
            pltpu.VMEM((Z - 1, M, CL), BF16),
            pltpu.VMEM((Z, M, CL), BF16),
            pltpu.VMEM((3, 3, C, 3 * CL), BF16),
            pltpu.VMEM((3, 9 * CL, C), BF16),
            pltpu.VMEM((2, CL * 8, W), F32),
            dma((7,)),
            dma((10,)),
            dma((2, Z - 1, 2)), dma((2 * Z - 1, 2)),
            dma((2, Z - 1)), dma((2 * Z - 1,)),
            dma((Z,)), dma((Z,)),
            dma((2,)), dma((2,)),
            dma((R,)), dma((R,)),
            dma((2, 2)), dma((2, 2)),
            dma((2, 2)), dma((2, 2)),
            dma((R,)), dma((R,)),
            dma((2, Z)), dma((2, Z)),
            dma((2,)),
        ],
        compiler_params=pltpu.CompilerParams(
            collective_id=0, has_side_effects=True, vmem_limit_bytes=40 * 1024 * 1024
        ),
    )(*(pltpu.with_memory_space_constraint(v, pltpu.HBM) for v in (
        latents.reshape(CL * T, W),
        cache_one.reshape(CL * 2, W),
        cache_two.reshape(CL * 2, W),
        gain_one.reshape(1, CL),
        bias_one.reshape(1, CL),
        gain_two.reshape(1, CL),
        bias_two.reshape(1, CL),
        weight_one,
        weight_two.reshape(3, 9 * CL, C),
    )))
    return out.reshape(CL, T, 2, 2, W).transpose(0, 1, 3, 2, 4).reshape(CL, T, 2, 2 * W)


def solution(mesh):
    return jax.shard_map(
        body,
        mesh=mesh,
        in_specs=(
            P("chan", None, "rows", None),
            P("chan", None, "rows", None),
            P("chan", None, "rows", None),
            P("chan"),
            P("chan"),
            P(None, None, None, None, "chan"),
            P("chan"),
            P("chan"),
            P(None, None, None, "chan", None),
        ),
        out_specs=P("chan", None, "rows", None),
        check_vma=False,
    )
```

```python
import functools

import jax
import jax.numpy as jnp
from jax import lax
from jax.experimental import pallas as pl
from jax.experimental.pallas import tpu as pltpu
from jax.sharding import PartitionSpec as P

CHANNELS = 512
GROUPS = 32
MESH = pl.DeviceIdType.MESH
F32 = jnp.float32
BF16 = jnp.bfloat16


epsilon = 1e-06


def padded(block, sides, width):
    for axis, dim in sides:
        count = lax.axis_size(axis)
        forward = [(i, i + 1) for i in range(count - 1)]
        backward = [(target, source) for source, target in forward]
        low = lax.ppermute(
            lax.slice_in_dim(block, block.shape[dim] - width, None, axis=dim), axis, forward
        )
        high = lax.ppermute(lax.slice_in_dim(block, 0, width, axis=dim), axis, backward)
        block = jnp.concatenate([low, block, high], axis=dim)
    return block


def group_silu(values, gain, bias):
    group_size = CHANNELS // GROUPS
    grouped = values.reshape(values.shape[0] // group_size, -1)
    sums, squares = lax.psum((jnp.sum(grouped, axis=1), jnp.sum(grouped * grouped, axis=1)), "rows")
    members = grouped.shape[1] * lax.axis_size("rows")
    average = sums / members
    spread = squares / members - average * average
    normed = ((grouped - average[:, None]) * lax.rsqrt(spread + epsilon)[:, None]).reshape(
        values.shape
    )
    scaled = normed * gain[:, None, None, None] + bias[:, None, None, None]
    return jax.nn.silu(scaled).astype(jnp.bfloat16)


def pad_rows(frames):
    return padded(frames, (("rows", 2),), 1)


def conv_block(frames, kernel):
    result = lax.conv_general_dilated(
        frames[None],
        kernel,
        (1, 1, 1),
        ((0, 0), (0, 0), (1, 1)),
        dimension_numbers=("NCDHW", "DHWIO", "NCDHW"),
        preferred_element_type=jnp.float32,
    )
    return result[0]


def gathered_conv(frames, kernel):
    channels = lax.all_gather(frames, "chan", axis=0, tiled=True)
    return conv_block(channels, kernel)


def plain_body(
    latents, cache_one, cache_two, gain_one, bias_one, weight_one, gain_two, bias_two, weight_two
):
    floats = latents.astype(jnp.float32)
    first = group_silu(floats, gain_one, bias_one)
    frames_one = pad_rows(jnp.concatenate([cache_one, first], axis=1))
    middle = gathered_conv(frames_one, weight_one).astype(jnp.bfloat16)
    second = group_silu(middle.astype(jnp.float32), gain_two, bias_two)
    frames_two = pad_rows(jnp.concatenate([cache_two, second], axis=1))
    columns = lax.all_to_all(weight_two, "chan", split_axis=4, concat_axis=3, tiled=True)
    result = floats + gathered_conv(frames_two, columns)
    return jnp.repeat(jnp.repeat(result, 2, axis=2), 2, axis=3)


def block_kernel(
    R, Z, CL, T, W,
    lat_hbm, c1_hbm, c2_hbm, g1_hbm, b1_hbm, g2_hbm, b2_hbm, w1_hbm, w2_hbm,
    out_ref,
    lat_v, c_v, gb,
    tmp, lat_t, raw, xc, xs1, xsc, acc1, part_out, part_in, mid, mid_in, x2, xs2, acc2,
    st1, st2, coef, rs_out, rs_in, w1, w2,
    isem, wsem, ls, lr, lr3, cs, cr, ss, kr, s1r, s2r, ns, hr, pr, mr, rsr,
):
    row = lax.axis_index("rows")
    me = lax.axis_index("chan")
    M = T * W
    C2 = 2 * W
    H = M // 2
    HL = CL * T // 2
    OWN = Z - 1
    has_up = row > 0
    has_down = row < R - 1
    edge = jnp.logical_or(me == 0, me == Z - 1)
    inner = jnp.logical_not(edge)
    is_inner = ((me + 1) // 2) % 2

    def partner(k):
        other = me * 0
        bit = 1
        while bit < Z:
            mine = (me // bit) % 2
            other = other + bit * ((1 - mine) if k & bit else mine)
            bit *= 2
        return other

    barrier = pltpu.get_barrier_semaphore()
    for k in range(1, R):
        pl.semaphore_signal(barrier, inc=1, device_id={"rows": lax.rem(row + k, R)}, device_id_type=MESH)
    for k in range(1, Z):
        pl.semaphore_signal(barrier, inc=1, device_id={"chan": partner(k)}, device_id_type=MESH)

    lat_load = pltpu.make_async_copy(lat_hbm, lat_v, isem.at[0])
    loads = [
        lat_load,
        pltpu.make_async_copy(c1_hbm, c_v.at[0], isem.at[1]),
        pltpu.make_async_copy(c2_hbm, c_v.at[1], isem.at[1]),
    ] + [
        pltpu.make_async_copy(v, gb.at[pl.ds(i, 1)], isem.at[2])
        for i, v in enumerate((g1_hbm, b1_hbm, g2_hbm, b2_hbm))
    ]
    place = (0, 2, 1)
    w_copies = []
    for dt in range(3):
        for dh in range(3):
            w_copies.append(
                pltpu.make_async_copy(
                    w1_hbm.at[dt, dh],
                    w1.at[dt, :, :, pl.ds(place[dh] * CL, CL)],
                    wsem.at[0],
                )
            )
    w2_copy = pltpu.make_async_copy(w2_hbm, w2, wsem.at[1])
    for copy in loads:
        copy.start()

    def wait_all(whole, sem):
        pltpu.make_async_copy(whole, whole, sem).wait()

    def to_chan(src, dst, send, recv, k):
        return pltpu.make_async_remote_copy(
            src_ref=src, dst_ref=dst, send_sem=send, recv_sem=recv,
            device_id={"chan": partner(k)}, device_id_type=MESH,
        )

    def to_row(src, dst, send, recv, k):
        return pltpu.make_async_remote_copy(
            src_ref=src, dst_ref=dst, send_sem=send, recv_sem=recv,
            device_id={"rows": lax.rem(row + k, R)}, device_id_type=MESH,
        )

    def along(src, buffer, send, recv, d, part, side):
        slot = OWN - side * d
        return pltpu.make_async_remote_copy(
            src_ref=src, dst_ref=buffer.at[(slot - side, *part)],
            send_sem=send, recv_sem=recv,
            device_id={"chan": me + side}, device_id_type=MESH,
        )

    def latent_hop(d, ch, side):
        slot = OWN - side * d
        rows = pl.ds(ch * HL, HL)
        src = lat_hbm.at[rows] if d == 0 else raw.at[slot, rows]
        way = (side + 1) // 2
        arrival = lr.at[way, d, ch] if d < 2 else lr3.at[way]
        return along(
            src, raw, ls.at[(side + 1) // 2, ch], arrival, d, (rows,), side
        )

    def cache_hop(d, side):
        slot = OWN - side * d
        return along(
            xc.at[slot], xc, cs.at[(side + 1) // 2], cr.at[(side + 1) // 2, d], d, (), side
        )

    def arrives(d, side):
        return me >= d if side > 0 else me + d <= Z - 1

    def goes(d, side):
        return jnp.logical_and(arrives(d, side), me < Z - 1 if side > 0 else me > 0)

    def also(here, some):
        return here if some is None else jnp.logical_and(here, some)

    def start_hop(hop, d, some=None):
        for side in (1, -1):

            @pl.when(also(goes(d, side), some))
            def _():
                if d > 0:
                    hop(d - 1, side).wait_send()
                hop(d, side).start()

    def wait_hop(hop, d, some=None):
        for side in (1, -1):

            @pl.when(also(arrives(d, side), some))
            def _():
                hop(d - 1, side).wait_recv()

    def wait_sent(hop, d, last=False):
        for side in (1, -1):
            here = goes(d, side)
            if last and d < Z - 2:
                here = jnp.logical_and(here, jnp.logical_not(goes(d + 1, side)))

            @pl.when(here)
            def _():
                hop(d, side).wait_send()

    def pass_on(hop, d, some=None):
        wait_hop(hop, d, some)
        if d < Z - 1:
            start_hop(hop, d, some)

    def latent_part(ch):
        return lambda d, side: latent_hop(d, ch, side)

    members = F32(R * M * (CHANNELS // GROUPS))
    gi = lax.broadcasted_iota(jnp.int32, (CL, CL), 0) // (CHANNELS // GROUPS)
    gj = lax.broadcasted_iota(jnp.int32, (CL, CL), 1) // (CHANNELS // GROUPS)
    same_group = (gi == gj).astype(BF16)

    def exact_dot(values, ones):
        terms = []
        for _ in range(3):
            terms.append(values.astype(BF16))
            values = values - terms[-1].astype(F32)
        count = terms[0].shape[0]
        out = jnp.dot(jnp.concatenate(terms, axis=0), ones, preferred_element_type=F32)
        return out[0:count] + out[count : 2 * count] + out[2 * count :]

    which = lax.broadcasted_iota(jnp.int32, (8, CL), 0)

    def local_stats(values):
        sums = jnp.sum(values, axis=0, keepdims=True)
        squares = jnp.sum(values * values, axis=0, keepdims=True)
        return jnp.where(which == 0, sums, jnp.where(which == 1, squares, 0.0))

    def share_stats(st, send, recv):
        for k in range(1, R):
            to_row(st.at[0], st.at[k], send, recv, k).start()

    def finish_stats(st, send, recv, gain):
        wait_all(st.at[pl.ds(1, R - 1)], recv)
        wait_all(st.at[pl.ds(1, R - 1)], send)
        total = st[0]
        for k in range(1, R):
            total = total + st[k]
        total = exact_dot(total, same_group) / members
        mean = total[0:1, :]
        spread = jnp.maximum(total[1:2, :] - mean * mean, 0.0)
        return mean, lax.rsqrt(spread + epsilon) * gain

    def normed(values, coefs):
        mean, scale, bias = coefs
        u = (values - mean) * scale + bias
        return (u / (1.0 + jnp.exp(-u))).astype(BF16)

    def shifted(block):
        rows = block.shape[0]
        cell = lax.broadcasted_iota(jnp.int32, (rows, CL), 0) % W
        wide = block.astype(F32)
        left = jnp.where(cell == 0, 0.0, pltpu.roll(wide, 1, 0)).astype(BF16)
        right = jnp.where(cell == W - 1, 0.0, pltpu.roll(wide, rows - 1, 0)).astype(BF16)
        return left, block, right

    def put(dst, rows, column, block):
        for dx, value in enumerate(shifted(block)):
            dst[rows, column + dx * CL : column + (dx + 1) * CL] = value

    with jax.named_scope("barrier wait"):
        pl.semaphore_wait(barrier, R - 1 + Z - 1)

    start_hop(latent_part(0), 0)
    for copy in w_copies:
        copy.start()

    halo_down = to_row(x2.at[1], x2.at[0], ns.at[0], hr.at[0], 1)
    halo_up = to_row(x2.at[1], x2.at[2], ns.at[1], hr.at[1], R - 1)

    with jax.named_scope("own latents"):
        lat_load.wait()
        tmp[...] = lat_v[...].astype(F32)
        for t in range(T):
            lat_t[t * W : (t + 1) * W, :] = tmp[pl.ds(t, CL, stride=T), :].T
        st1[0] = local_stats(lat_t[...])
        share_stats(st1, ss.at[0], s1r.at[0])

    with jax.named_scope("own caches"):
        wait_all(c_v, isem.at[1])
        for i, (buffer, slot) in enumerate(((xc, OWN), (x2, 1))):
            tmp[0 : 2 * CL, :] = c_v[i].astype(F32)
            for t in range(2):
                buffer[slot, t * W : (t + 1) * W, :] = (
                    tmp[pl.ds(t, CL, stride=2), :].T.astype(BF16)
                )
        acc1[...] = jnp.zeros_like(acc1)

    start_hop(latent_part(1), 0)

    @pl.when(has_down)
    def _():
        halo_down.start()

    @pl.when(has_up)
    def _():
        halo_up.start()

    def kernel_one(dt, z, low, high):
        base = pl.ds(pl.multiple_of(z * CL, CL), CL)
        return jnp.concatenate([w1[dt, dx, base, low:high] for dx in range(3)], axis=0)

    def latent_dots(z):
        for dt in (2, 1, 0):
            start = (2 - dt) * W
            acc1[start:, :] += jnp.dot(
                xs1[0 : M - start, :], kernel_one(dt, z, 0, 3 * CL), preferred_element_type=F32
            )

    def last_latent_dots(z, half):
        for dt in (2, 1, 0):
            first = half * H - (2 - dt) * W
            skip = max(0, -first)
            if skip < H:
                acc1[half * H + skip : (half + 1) * H, :] += jnp.dot(
                    xs1[first + skip : first + H, :], kernel_one(dt, z, 0, 3 * CL),
                    preferred_element_type=F32,
                )

    def cache_dots(z, low, high):
        for dt in range(2):
            acc1[0 : C2 - dt * W, low:high] += jnp.dot(
                xsc[dt * W : C2, :], kernel_one(dt, z, low, high), preferred_element_type=F32
            )

    def place_caches(slot):
        for t in range(2):
            rows = slice(t * W, (t + 1) * W)
            put(xsc, rows, 0, xc[slot, rows, :])

    def place_latents(slot, coefs):
        tmp[...] = raw[slot].astype(F32)
        for t in range(T):
            put(
                xs1, slice(t * W, (t + 1) * W), 0,
                normed(tmp[pl.ds(t, CL, stride=T), :].T, coefs),
            )

    def plane(k):
        if k == 1:
            return partner(1), 1
        a, b = partner(2), partner(3)
        if k == 2:
            return a + is_inner * (b - a), 2 + is_inner
        return b + is_inner * (a - b), 3 - is_inner

    def place_other(k):
        z, at = plane(k)
        place_latents(OWN + z - me, tuple(coef[at, i : i + 1, :] for i in range(3)))
        return z

    def other_latents(k):
        latent_dots(place_other(k))

    wait_all(w1, wsem.at[0])
    w2_copy.start()
    with jax.named_scope("own cache dots"):
        place_caches(OWN)
        cache_dots(me, 0, 3 * CL)
    start_hop(cache_hop, 0)

    with jax.named_scope("stats one"):
        wait_all(gb.at[pl.ds(0, 4)], isem.at[2])
        mean, scale = finish_stats(st1, ss.at[0], s1r.at[0], gb[0:1, :])
        bias = gb[1:2, :]
        coef[0] = jnp.where(which == 0, mean, jnp.where(which == 1, scale, bias))
        for k in range(1, Z):
            to_chan(coef.at[0], coef.at[k], ss.at[0], kr.at[0], k).start()

    with jax.named_scope("latents 1, part 0"):
        pass_on(latent_part(0), 1)

    with jax.named_scope("own latent dots"):
        for t in range(T):
            rows = slice(t * W, (t + 1) * W)
            put(xs1, rows, 0, normed(lat_t[rows, :], (mean, scale, bias)))
        latent_dots(me)
    with jax.named_scope("latents 1, part 1"):
        pass_on(latent_part(1), 1)
    with jax.named_scope("conv2 of caches"):
        w2_copy.wait()

        @pl.when(has_up)
        def _():
            halo_down.wait_recv()

        @pl.when(has_down)
        def _():
            halo_up.wait_recv()

        @pl.when(jnp.logical_not(has_up))
        def _():
            x2[0] = jnp.zeros((C2, CL), BF16)
            xs2[C2:, 0 : 3 * CL] = jnp.zeros((M, 3 * CL), BF16)

        @pl.when(jnp.logical_not(has_down))
        def _():
            x2[2] = jnp.zeros((C2, CL), BF16)
            xs2[C2:, 6 * CL :] = jnp.zeros((M, 3 * CL), BF16)

        for dh in range(3):
            put(xs2, slice(0, C2), dh * 3 * CL, x2[dh])
        both = jnp.dot(xs2[0:C2, :], w2[0], preferred_element_type=F32)
        one = jnp.dot(xs2[W:C2, :], w2[1], preferred_element_type=F32)
        for d in range(Z):
            cols = slice(d * CL, (d + 1) * CL)
            acc2[d, 0:W] = both[0:W, cols] + one[:, cols]
            acc2[d, W:C2] = both[W:C2, cols]
    with jax.named_scope("caches 1"):
        pass_on(cache_hop, 1)
    with jax.named_scope("latents 2, part 0"):
        pass_on(latent_part(0), 2)
    with jax.named_scope("latent dots 1"):
        wait_all(coef.at[pl.ds(1, Z - 1)], kr.at[0])
        other_latents(1)
    with jax.named_scope("latents 2, part 1"):
        pass_on(latent_part(1), 2)
    with jax.named_scope("latent dots 2"):
        other_latents(2)
    with jax.named_scope("caches 2"):
        pass_on(cache_hop, 2)
    with jax.named_scope("cache dots 1"):
        z, _ = plane(1)
        place_caches(OWN + z - me)
        cache_dots(z, 0, 3 * CL)
    with jax.named_scope("cache dots 2"):
        z, _ = plane(2)
        place_caches(OWN + z - me)
        cache_dots(z, 0, 3 * CL)

    with jax.named_scope("latents 3"):
        for side in (1, -1):

            @pl.when(arrives(Z - 1, side))
            def _():
                wait_all(raw.at[OWN - side * (Z - 1)], lr3.at[(side + 1) // 2])

    def rows_of(half):
        return slice(half * H, (half + 1) * H)

    def part_copies(half):
        rows = rows_of(half)
        return (
            to_row(part_out.at[0, rows], part_in.at[0, rows], ns.at[2 - 2 * half], pr.at[0, half], 1),
            to_row(part_out.at[1, rows], part_in.at[1, rows], ns.at[3 - 2 * half], pr.at[1, half], R - 1),
        )

    def mid_copies(half):
        rows = rows_of(half)
        recv = hr if half else mr
        return (
            to_row(mid.at[rows], mid_in.at[0, rows], ns.at[0], recv.at[0], 1),
            to_row(mid.at[rows], mid_in.at[1, rows], ns.at[1], recv.at[1], R - 1),
        )

    def start_rows(copies, before=()):
        for have, copy, old in zip((has_down, has_up), copies, before or (None, None)):

            @pl.when(have)
            def _():
                if old is not None:
                    old.wait_send()
                copy.start()

    def send_parts(half):
        rows = rows_of(half)
        part_out[0, rows] = acc1[rows, 0:CL].astype(BF16)
        part_out[1, rows] = acc1[rows, CL : 2 * CL].astype(BF16)
        start_rows(part_copies(half), (halo_down, halo_up) if half else ())

    def finish_mid(half):
        rows = rows_of(half)
        down, up = part_copies(half)

        @pl.when(has_up)
        def _():
            down.wait_recv()
            acc1[rows, 2 * CL :] += part_in[0, rows].astype(F32)

        @pl.when(has_down)
        def _():
            up.wait_recv()
            acc1[rows, 2 * CL :] += part_in[1, rows].astype(F32)

        mid[rows] = acc1[rows, 2 * CL :].astype(BF16)
        return local_stats(mid[rows].astype(F32))

    with jax.named_scope("parts of half 1"):
        z = place_other(3)
        last_latent_dots(z, 1)
        send_parts(1)
    with jax.named_scope("latent dots 3"):
        last_latent_dots(z, 0)
    with jax.named_scope("caches 3"):
        pass_on(cache_hop, 3)
    with jax.named_scope("cache dots 3"):
        z, _ = plane(3)
        place_caches(OWN + z - me)
        cache_dots(z, 0, 3 * CL)
        send_parts(0)
    with jax.named_scope("mid of half 1"):
        partial = finish_mid(1)
        start_rows(mid_copies(1), part_copies(1))

    with jax.named_scope("mid of half 0"):
        st2[0] = partial + finish_mid(0)
        wait_all(coef.at[pl.ds(1, Z - 1)], ss.at[0])
        share_stats(st2, ss.at[0], s2r.at[0])
        start_rows(mid_copies(0))
        for hop in (latent_part(0), latent_part(1), cache_hop):
            for d in range(Z - 1):
                wait_sent(hop, d, last=True)
    with jax.named_scope("stats two"):
        coefs_two = (*finish_stats(st2, ss.at[0], s2r.at[0], gb[2:3, :]), gb[3:4, :])

    def place_mid(half):
        rows = rows_of(half)
        there = slice(C2 + half * H, C2 + (half + 1) * H)
        put(xs2, there, 3 * CL, normed(mid[rows].astype(F32), coefs_two))
        down, up = mid_copies(half)

        @pl.when(has_up)
        def _():
            down.wait_recv()
            put(xs2, there, 0, normed(mid_in[0, rows].astype(F32), coefs_two))

        @pl.when(has_down)
        def _():
            up.wait_recv()
            put(xs2, there, 6 * CL, normed(mid_in[1, rows].astype(F32), coefs_two))

    ZH = Z // 2
    mine = me // ZH

    def second_dots(half, pair):
        cols = pl.ds(pl.multiple_of(pair * (ZH * CL), ZH * CL), ZH * CL)
        for dt in (2, 1, 0):
            first = half * H - (2 - dt) * W
            skip = max(0, -first)
            if skip >= H:
                continue
            term = jnp.dot(
                xs2[C2 + first + skip : C2 + first + H, :], w2[dt, :, cols],
                preferred_element_type=F32,
            )
            for j in range(ZH):
                rows = slice(half * H + skip, (half + 1) * H)
                cut = term[:, j * CL : (j + 1) * CL]
                if half > 0 and dt == 2:
                    acc2[pair * ZH + j, rows] = cut
                else:
                    acc2[pair * ZH + j, rows] += cut

    def sum_copy(slot, half, k, to):
        rows = rows_of(half)
        return to_chan(
            rs_out.at[k - 1, rows], rs_in.at[slot, rows],
            cs.at[half] if k == Z - 1 else ls.at[half, k - 1], rsr.at[half, slot], to,
        )

    def send_sum(half, k, slot, to):
        rows = rows_of(half)
        rs_out[k - 1, rows] = acc2[partner(k), rows].astype(BF16)
        sum_copy(slot, half, k, to).start()

    MERGE = 0

    def send_merged(half):
        rows = rows_of(half)
        sum_copy(MERGE, half, 3, 1).wait_recv()
        rs_out[1, rows] = (acc2[partner(2), rows] + rs_in[MERGE, rows].astype(F32)).astype(BF16)
        sum_copy(2, half, 2, 2).start()

    with jax.named_scope("place half 0"):
        place_mid(0)
    with jax.named_scope("conv2 half 0 far"):
        second_dots(0, 1 - mine)

        @pl.when(edge)
        def _():
            send_sum(0, 3, MERGE, 1)

        @pl.when(inner)
        def _():
            send_sum(0, 3, 3, 3)

    with jax.named_scope("place half 1"):
        place_mid(1)
    with jax.named_scope("conv2 half 1 far"):
        second_dots(1, 1 - mine)

        @pl.when(edge)
        def _():
            send_sum(1, 3, MERGE, 1)

        @pl.when(inner)
        def _():
            send_sum(1, 3, 3, 3)

    with jax.named_scope("conv2 half 0 near"):
        second_dots(0, mine)

        @pl.when(edge)
        def _():
            send_sum(0, 2, 2, 2)

        @pl.when(inner)
        def _():
            send_sum(0, 1, 1, 1)
            send_merged(0)

    with jax.named_scope("conv2 half 1 near"):
        second_dots(1, mine)

        @pl.when(edge)
        def _():
            send_sum(1, 2, 2, 2)

        @pl.when(inner)
        def _():
            send_sum(1, 1, 1, 1)

        lat_t[...] = lat_t[...] + acc2[me]
    with jax.named_scope("last sums out"):

        @pl.when(edge)
        def _():
            sum_copy(2, 0, 2, 2).wait_send()
            send_sum(0, 1, 1, 1)
            sum_copy(2, 1, 2, 2).wait_send()
            sum_copy(1, 0, 1, 1).wait_send()
            send_sum(1, 1, 1, 1)

        @pl.when(inner)
        def _():
            send_merged(1)

    ei = lax.broadcasted_iota(jnp.int32, (W, 2 * W), 0)
    ej = lax.broadcasted_iota(jnp.int32, (W, 2 * W), 1) // 2
    twice = (ei == ej).astype(BF16)

    for half in range(2):
        rows = rows_of(half)
        with jax.named_scope(f"sums wait {half}"):
            sum_copy(1, half, 1, 1).wait_recv()
            sum_copy(2, half, 2, 2).wait_recv()

            @pl.when(inner)
            def _():
                sum_copy(3, half, 3, 3).wait_recv()
                lat_t[rows, :] += rs_in[3, rows].astype(F32)

        with jax.named_scope(f"upsample {half}"):
            for t in range(half * T // 2, (half + 1) * T // 2):
                rows = slice(t * W, (t + 1) * W)
                total = lat_t[rows, :] + rs_in[1, rows].astype(F32) + rs_in[2, rows].astype(F32)
                wide = exact_dot(total.T, twice)
                for side in range(2):
                    for again in range(2):
                        out_ref[pl.ds(t * 4 + side * 2 + again, CL, stride=4 * T), :] = wide[
                            :, side * W : (side + 1) * W
                        ]

    with jax.named_scope("sends wait"):
        for half in range(2):
            sum_copy(1, half, 3, 1).wait_send()
        sum_copy(1, 1, 1, 1).wait_send()

        @pl.when(inner)
        def _():
            sum_copy(1, 0, 1, 1).wait_send()
            for half in range(2):
                sum_copy(2, half, 2, 2).wait_send()

        for have, way in ((has_down, 0), (has_up, 1)):

            @pl.when(have)
            def _():
                part_copies(0)[way].wait_send()
                wait_all(mid, ns.at[way])


def body(
    latents, cache_one, cache_two, gain_one, bias_one, weight_one, gain_two, bias_two, weight_two
):
    CL, T, rows_here, W = latents.shape
    R, Z = lax.axis_size("rows"), lax.axis_size("chan")
    if CL != 128 or W != 128 or rows_here != 1 or T != 4 or R < 2 or Z != 4:
        return plain_body(
            latents, cache_one, cache_two, gain_one, bias_one, weight_one, gain_two, bias_two,
            weight_two,
        )
    C = CL * Z
    M = T * W
    hbm = pl.BlockSpec(memory_space=pltpu.HBM)
    dma = pltpu.SemaphoreType.DMA
    out = pl.pallas_call(
        functools.partial(block_kernel, R, Z, CL, T, W),
        out_shape=jax.ShapeDtypeStruct((CL * T * 4, W), F32),
        in_specs=[hbm] * 9,
        out_specs=pl.BlockSpec(memory_space=pltpu.VMEM),
        scratch_shapes=[
            pltpu.VMEM((CL * T, W), BF16),
            pltpu.VMEM((2, CL * 2, W), BF16),
            pltpu.VMEM((8, CL), F32),
            pltpu.VMEM((CL * T, W), F32),
            pltpu.VMEM((M, CL), F32),
            pltpu.VMEM((2 * Z - 1, CL * T, W), BF16),
            pltpu.VMEM((2 * Z - 1, 2 * W, CL), BF16),
            pltpu.VMEM((M, 3 * CL), BF16),
            pltpu.VMEM((2 * W, 3 * CL), BF16),
            pltpu.VMEM((M, 3 * CL), F32),
            pltpu.VMEM((2, M, CL), BF16),
            pltpu.VMEM((2, M, CL), BF16),
            pltpu.VMEM((M, CL), BF16),
            pltpu.VMEM((2, M, CL), BF16),
            pltpu.VMEM((3, 2 * W, CL), BF16),
            pltpu.VMEM((M + 2 * W, 9 * CL), BF16),
            pltpu.VMEM((Z, M, CL), F32),
            pltpu.VMEM((R, 8, CL), F32),
            pltpu.VMEM((R, 8, CL), F32),
            pltpu.VMEM((Z, 8, CL), F32),
            pltpu.VMEM((Z - 1, M, CL), BF16),
            pltpu.VMEM((Z, M, CL), BF16),
            pltpu.VMEM((3, 3, C, 3 * CL), BF16),
            pltpu.VMEM((3, 9 * CL, C), BF16),
            dma((3,)), dma((2,)),
            dma((2, 2)), dma((2, 2, 2)), dma((2,)),
            dma((2,)), dma((2, Z - 1)),
            dma((1,)), dma((1,)), dma((1,)), dma((1,)),
            dma((4,)), dma((2,)), dma((2, 2)), dma((2,)),
            dma((2, Z)),
        ],
        compiler_params=pltpu.CompilerParams(
            collective_id=0, has_side_effects=True, vmem_limit_bytes=40 * 1024 * 1024
        ),
    )(*(pltpu.with_memory_space_constraint(v, pltpu.HBM) for v in (
        latents.reshape(CL * T, W),
        cache_one.reshape(CL * 2, W),
        cache_two.reshape(CL * 2, W),
        gain_one.reshape(1, CL),
        bias_one.reshape(1, CL),
        gain_two.reshape(1, CL),
        bias_two.reshape(1, CL),
        weight_one,
        weight_two.reshape(3, 9 * CL, C),
    )))
    return out.reshape(CL, T, 2, 2, W).transpose(0, 1, 3, 2, 4).reshape(CL, T, 2, 2 * W)


def solution(mesh):
    return jax.shard_map(
        body,
        mesh=mesh,
        in_specs=(
            P("chan", None, "rows", None),
            P("chan", None, "rows", None),
            P("chan", None, "rows", None),
            P("chan"),
            P("chan"),
            P(None, None, None, None, "chan"),
            P("chan"),
            P("chan"),
            P(None, None, None, "chan", None),
        ),
        out_specs=P("chan", None, "rows", None),
        check_vma=False,
    )
```

```python
import functools

import jax
import jax.numpy as jnp
from jax import lax
from jax.experimental import pallas as pl
from jax.experimental.pallas import tpu as pltpu
from jax.sharding import PartitionSpec as P

CHANNELS = 512
GROUPS = 32
MESH = pl.DeviceIdType.MESH
F32 = jnp.float32
BF16 = jnp.bfloat16


epsilon = 1e-06


def padded(block, sides, width):
    for axis, dim in sides:
        count = lax.axis_size(axis)
        forward = [(i, i + 1) for i in range(count - 1)]
        backward = [(target, source) for source, target in forward]
        low = lax.ppermute(
            lax.slice_in_dim(block, block.shape[dim] - width, None, axis=dim), axis, forward
        )
        high = lax.ppermute(lax.slice_in_dim(block, 0, width, axis=dim), axis, backward)
        block = jnp.concatenate([low, block, high], axis=dim)
    return block


def group_silu(values, gain, bias):
    group_size = CHANNELS // GROUPS
    grouped = values.reshape(values.shape[0] // group_size, -1)
    sums, squares = lax.psum((jnp.sum(grouped, axis=1), jnp.sum(grouped * grouped, axis=1)), "rows")
    members = grouped.shape[1] * lax.axis_size("rows")
    average = sums / members
    spread = squares / members - average * average
    normed = ((grouped - average[:, None]) * lax.rsqrt(spread + epsilon)[:, None]).reshape(
        values.shape
    )
    scaled = normed * gain[:, None, None, None] + bias[:, None, None, None]
    return jax.nn.silu(scaled).astype(jnp.bfloat16)


def pad_rows(frames):
    return padded(frames, (("rows", 2),), 1)


def conv_block(frames, kernel):
    result = lax.conv_general_dilated(
        frames[None],
        kernel,
        (1, 1, 1),
        ((0, 0), (0, 0), (1, 1)),
        dimension_numbers=("NCDHW", "DHWIO", "NCDHW"),
        preferred_element_type=jnp.float32,
    )
    return result[0]


def gathered_conv(frames, kernel):
    channels = lax.all_gather(frames, "chan", axis=0, tiled=True)
    return conv_block(channels, kernel)


def plain_body(
    latents, cache_one, cache_two, gain_one, bias_one, weight_one, gain_two, bias_two, weight_two
):
    floats = latents.astype(jnp.float32)
    first = group_silu(floats, gain_one, bias_one)
    frames_one = pad_rows(jnp.concatenate([cache_one, first], axis=1))
    middle = gathered_conv(frames_one, weight_one).astype(jnp.bfloat16)
    second = group_silu(middle.astype(jnp.float32), gain_two, bias_two)
    frames_two = pad_rows(jnp.concatenate([cache_two, second], axis=1))
    columns = lax.all_to_all(weight_two, "chan", split_axis=4, concat_axis=3, tiled=True)
    result = floats + gathered_conv(frames_two, columns)
    return jnp.repeat(jnp.repeat(result, 2, axis=2), 2, axis=3)


def block_kernel(
    R, Z, CL, T, W,
    lat_hbm, c1_hbm, c2_hbm, g1_hbm, b1_hbm, g2_hbm, b2_hbm, w1_hbm, w2_hbm,
    out_ref,
    lat_v, c_v, gb,
    tmp, lat_t, raw, xc, xs1, xsc, acc1, part_out, part_in, mid, mid_in, x2, xs2, acc2,
    st1, st2, coef, rs_out, rs_in, w1, w2,
    isem, wsem, ls, lr, lr3, cs, cr, ss, kr, s1r, s2r, ns, hr, pr, mr, rsr, rf,
):
    row = lax.axis_index("rows")
    me = lax.axis_index("chan")
    M = T * W
    C2 = 2 * W
    H = M // 2
    HL = CL * T // 2
    OWN = Z - 1
    has_up = row > 0
    has_down = row < R - 1
    edge = jnp.logical_or(me == 0, me == Z - 1)
    inner = jnp.logical_not(edge)
    is_inner = ((me + 1) // 2) % 2

    def partner(k):
        other = me * 0
        bit = 1
        while bit < Z:
            mine = (me // bit) % 2
            other = other + bit * ((1 - mine) if k & bit else mine)
            bit *= 2
        return other

    st1[...] = jnp.zeros_like(st1)
    st2[...] = jnp.zeros_like(st2)
    barrier = pltpu.get_barrier_semaphore()
    for k in range(1, R):
        pl.semaphore_signal(barrier, inc=1, device_id={"rows": lax.rem(row + k, R)}, device_id_type=MESH)
    for k in range(1, Z):
        pl.semaphore_signal(barrier, inc=1, device_id={"chan": partner(k)}, device_id_type=MESH)

    lat_load = pltpu.make_async_copy(lat_hbm, lat_v, isem.at[0])
    loads = [
        lat_load,
        pltpu.make_async_copy(c1_hbm, c_v.at[0], isem.at[1]),
        pltpu.make_async_copy(c2_hbm, c_v.at[1], isem.at[1]),
    ] + [
        pltpu.make_async_copy(v, gb.at[pl.ds(i, 1)], isem.at[2])
        for i, v in enumerate((g1_hbm, b1_hbm, g2_hbm, b2_hbm))
    ]
    place = (0, 2, 1)
    w_copies = []
    for dt in range(3):
        for dh in range(3):
            w_copies.append(
                pltpu.make_async_copy(
                    w1_hbm.at[dt, dh],
                    w1.at[dt, :, :, pl.ds(place[dh] * CL, CL)],
                    wsem.at[0],
                )
            )
    w2_copy = pltpu.make_async_copy(w2_hbm, w2, wsem.at[1])
    for copy in loads:
        copy.start()

    def wait_all(whole, sem):
        pltpu.make_async_copy(whole, whole, sem).wait()

    def to_chan(src, dst, send, recv, k):
        return pltpu.make_async_remote_copy(
            src_ref=src, dst_ref=dst, send_sem=send, recv_sem=recv,
            device_id={"chan": partner(k)}, device_id_type=MESH,
        )

    def to_row(src, dst, send, recv, k):
        return pltpu.make_async_remote_copy(
            src_ref=src, dst_ref=dst, send_sem=send, recv_sem=recv,
            device_id={"rows": lax.rem(row + k, R)}, device_id_type=MESH,
        )

    def along(src, buffer, send, recv, d, part, side):
        slot = OWN - side * d
        return pltpu.make_async_remote_copy(
            src_ref=src, dst_ref=buffer.at[(slot - side, *part)],
            send_sem=send, recv_sem=recv,
            device_id={"chan": me + side}, device_id_type=MESH,
        )

    def latent_hop(d, ch, side):
        slot = OWN - side * d
        rows = pl.ds(ch * HL, HL)
        src = lat_hbm.at[rows] if d == 0 else raw.at[slot, rows]
        way = (side + 1) // 2
        arrival = lr.at[way, d, ch] if d < 2 else lr3.at[way]
        return along(
            src, raw, ls.at[(side + 1) // 2, ch], arrival, d, (rows,), side
        )

    def cache_hop(d, side):
        slot = OWN - side * d
        return along(
            xc.at[slot], xc, cs.at[(side + 1) // 2], cr.at[(side + 1) // 2, d], d, (), side
        )

    def arrives(d, side):
        return me >= d if side > 0 else me + d <= Z - 1

    def goes(d, side):
        return jnp.logical_and(arrives(d, side), me < Z - 1 if side > 0 else me > 0)

    def also(here, some):
        return here if some is None else jnp.logical_and(here, some)

    def start_hop(hop, d, some=None):
        for side in (1, -1):

            @pl.when(also(goes(d, side), some))
            def _():
                if d > 0:
                    hop(d - 1, side).wait_send()
                hop(d, side).start()

    def wait_hop(hop, d, some=None):
        for side in (1, -1):

            @pl.when(also(arrives(d, side), some))
            def _():
                hop(d - 1, side).wait_recv()

    def wait_sent(hop, d, last=False):
        for side in (1, -1):
            here = goes(d, side)
            if last and d < Z - 2:
                here = jnp.logical_and(here, jnp.logical_not(goes(d + 1, side)))

            @pl.when(here)
            def _():
                hop(d, side).wait_send()

    def pass_on(hop, d, some=None):
        wait_hop(hop, d, some)
        if d < Z - 1:
            start_hop(hop, d, some)

    def latent_part(ch):
        return lambda d, side: latent_hop(d, ch, side)

    members = F32(R * M * (CHANNELS // GROUPS))
    gi = lax.broadcasted_iota(jnp.int32, (CL, CL), 0) // (CHANNELS // GROUPS)
    gj = lax.broadcasted_iota(jnp.int32, (CL, CL), 1) // (CHANNELS // GROUPS)
    same_group = (gi == gj).astype(BF16)

    def exact_dot(values, ones):
        terms = []
        for _ in range(3):
            terms.append(values.astype(BF16))
            values = values - terms[-1].astype(F32)
        count = terms[0].shape[0]
        out = jnp.dot(jnp.concatenate(terms, axis=0), ones, preferred_element_type=F32)
        return out[0:count] + out[count : 2 * count] + out[2 * count :]

    which = lax.broadcasted_iota(jnp.int32, (8, CL), 0)

    def local_stats(values):
        sums = jnp.sum(values, axis=0, keepdims=True)
        squares = jnp.sum(values * values, axis=0, keepdims=True)
        return jnp.where(which == 0, sums, jnp.where(which == 1, squares, 0.0))

    def share_stats(st, send, recv):
        for k in range(1, R):
            to_row(st.at[0, pl.ds(0, 2)], st.at[k, pl.ds(0, 2)], send, recv, k).start()

    def finish_stats(st, send, recv, gain):
        wait_all(st.at[pl.ds(1, R - 1), pl.ds(0, 2)], recv)
        wait_all(st.at[pl.ds(1, R - 1), pl.ds(0, 2)], send)
        total = st[0]
        for k in range(1, R):
            total = total + st[k]
        total = exact_dot(total, same_group) / members
        mean = total[0:1, :]
        spread = jnp.maximum(total[1:2, :] - mean * mean, 0.0)
        return mean, lax.rsqrt(spread + epsilon) * gain

    def normed(values, coefs):
        mean, scale, bias = coefs
        u = (values - mean) * scale + bias
        return (u / (1.0 + jnp.exp(-u))).astype(BF16)

    def shifted(block):
        rows = block.shape[0]
        cell = lax.broadcasted_iota(jnp.int32, (rows, CL), 0) % W
        wide = block.astype(F32)
        left = jnp.where(cell == 0, 0.0, pltpu.roll(wide, 1, 0)).astype(BF16)
        right = jnp.where(cell == W - 1, 0.0, pltpu.roll(wide, rows - 1, 0)).astype(BF16)
        return left, block, right

    def put(dst, rows, column, block):
        for dx, value in enumerate(shifted(block)):
            dst[rows, column + dx * CL : column + (dx + 1) * CL] = value

    with jax.named_scope("barrier wait"):
        pl.semaphore_wait(barrier, R - 1 + Z - 1)

    start_hop(latent_part(0), 0)
    for copy in w_copies:
        copy.start()

    halo_down = to_row(x2.at[1], x2.at[0], ns.at[0], hr.at[0], 1)
    halo_up = to_row(x2.at[1], x2.at[2], ns.at[1], hr.at[1], R - 1)

    with jax.named_scope("own latents"):
        lat_load.wait()
        tmp[...] = lat_v[...].astype(F32)
        for t in range(T):
            lat_t[t * W : (t + 1) * W, :] = tmp[pl.ds(t, CL, stride=T), :].T
        st1[0] = local_stats(lat_t[...])
        share_stats(st1, ss.at[0], s1r.at[0])

    with jax.named_scope("own caches"):
        wait_all(c_v, isem.at[1])
        for i, (buffer, slot) in enumerate(((xc, OWN), (x2, 1))):
            tmp[0 : 2 * CL, :] = c_v[i].astype(F32)
            for t in range(2):
                buffer[slot, t * W : (t + 1) * W, :] = (
                    tmp[pl.ds(t, CL, stride=2), :].T.astype(BF16)
                )
        acc1[...] = jnp.zeros_like(acc1)

    start_hop(latent_part(1), 0)

    @pl.when(has_down)
    def _():
        halo_down.start()

    @pl.when(has_up)
    def _():
        halo_up.start()

    def kernel_one(dt, z, low, high):
        base = pl.ds(pl.multiple_of(z * CL, CL), CL)
        return jnp.concatenate([w1[dt, dx, base, low:high] for dx in range(3)], axis=0)

    def latent_dots(z):
        for dt in (2, 1, 0):
            start = (2 - dt) * W
            acc1[start:, :] += jnp.dot(
                xs1[0 : M - start, :], kernel_one(dt, z, 0, 3 * CL), preferred_element_type=F32
            )

    def last_latent_dots(z, half, low, high):
        for dt in (2, 1, 0):
            first = half * H - (2 - dt) * W
            skip = max(0, -first)
            if skip < H:
                acc1[half * H + skip : (half + 1) * H, low:high] += jnp.dot(
                    xs1[first + skip : first + H, :], kernel_one(dt, z, low, high),
                    preferred_element_type=F32,
                )

    def cache_dots(z, low, high):
        for dt in range(2):
            acc1[0 : C2 - dt * W, low:high] += jnp.dot(
                xsc[dt * W : C2, :], kernel_one(dt, z, low, high), preferred_element_type=F32
            )

    def place_caches(slot):
        for t in range(2):
            rows = slice(t * W, (t + 1) * W)
            put(xsc, rows, 0, xc[slot, rows, :])

    def place_latents(slot, coefs):
        tmp[...] = raw[slot].astype(F32)
        for t in range(T):
            put(
                xs1, slice(t * W, (t + 1) * W), 0,
                normed(tmp[pl.ds(t, CL, stride=T), :].T, coefs),
            )

    def plane(k):
        if k == 1:
            return partner(1), 1
        a, b = partner(2), partner(3)
        if k == 2:
            return a + is_inner * (b - a), 2 + is_inner
        return b + is_inner * (a - b), 3 - is_inner

    def place_other(k):
        z, at = plane(k)
        place_latents(OWN + z - me, tuple(coef[at, i : i + 1, :] for i in range(3)))
        return z

    def other_latents(k):
        latent_dots(place_other(k))

    wait_all(w1, wsem.at[0])
    w2_copy.start()
    with jax.named_scope("own cache dots"):
        place_caches(OWN)
        cache_dots(me, 0, 3 * CL)
    start_hop(cache_hop, 0)

    with jax.named_scope("stats one"):
        wait_all(gb.at[pl.ds(0, 4)], isem.at[2])
        mean, scale = finish_stats(st1, ss.at[0], s1r.at[0], gb[0:1, :])
        bias = gb[1:2, :]
        coef[0] = jnp.where(which == 0, mean, jnp.where(which == 1, scale, bias))
        for k in range(1, Z):
            to_chan(coef.at[0], coef.at[k], ss.at[0], kr.at[0], k).start()

    with jax.named_scope("latents 1, part 0"):
        pass_on(latent_part(0), 1)

    with jax.named_scope("own latent dots"):
        for t in range(T):
            rows = slice(t * W, (t + 1) * W)
            put(xs1, rows, 0, normed(lat_t[rows, :], (mean, scale, bias)))
        latent_dots(me)
    with jax.named_scope("latents 1, part 1"):
        pass_on(latent_part(1), 1)
    with jax.named_scope("conv2 of caches"):
        w2_copy.wait()

        @pl.when(has_up)
        def _():
            halo_down.wait_recv()

        @pl.when(has_down)
        def _():
            halo_up.wait_recv()

        @pl.when(jnp.logical_not(has_up))
        def _():
            x2[0] = jnp.zeros((C2, CL), BF16)
            xs2[C2:, 0 : 3 * CL] = jnp.zeros((M, 3 * CL), BF16)

        @pl.when(jnp.logical_not(has_down))
        def _():
            x2[2] = jnp.zeros((C2, CL), BF16)
            xs2[C2:, 6 * CL :] = jnp.zeros((M, 3 * CL), BF16)

        for dh in range(3):
            put(xs2, slice(0, C2), dh * 3 * CL, x2[dh])
        both = jnp.dot(xs2[0:C2, :], w2[0], preferred_element_type=F32)
        one = jnp.dot(xs2[W:C2, :], w2[1], preferred_element_type=F32)
        for d in range(Z):
            cols = slice(d * CL, (d + 1) * CL)
            acc2[d, 0:W] = both[0:W, cols] + one[:, cols]
            acc2[d, W:C2] = both[W:C2, cols]
    with jax.named_scope("caches 1"):
        pass_on(cache_hop, 1)
    with jax.named_scope("latents 2, part 0"):
        pass_on(latent_part(0), 2)
    with jax.named_scope("latent dots 1"):
        wait_all(coef.at[pl.ds(1, Z - 1)], kr.at[0])
        other_latents(1)
    with jax.named_scope("latents 2, part 1"):
        pass_on(latent_part(1), 2)
    with jax.named_scope("latent dots 2"):
        other_latents(2)
    with jax.named_scope("caches 2"):
        pass_on(cache_hop, 2)
    with jax.named_scope("cache dots 1"):
        z, _ = plane(1)
        place_caches(OWN + z - me)
        cache_dots(z, 0, 3 * CL)
    with jax.named_scope("cache dots 2"):
        z, _ = plane(2)
        place_caches(OWN + z - me)
        cache_dots(z, 0, 3 * CL)

    with jax.named_scope("latents 3"):
        for side in (1, -1):

            @pl.when(arrives(Z - 1, side))
            def _():
                wait_all(raw.at[OWN - side * (Z - 1)], lr3.at[(side + 1) // 2])

    def rows_of(half):
        return slice(half * H, (half + 1) * H)

    def part_copies(half):
        rows = rows_of(half)
        return (
            to_row(part_out.at[0, rows], part_in.at[0, rows], ns.at[2 - 2 * half], pr.at[0, half], 1),
            to_row(part_out.at[1, rows], part_in.at[1, rows], ns.at[3 - 2 * half], pr.at[1, half], R - 1),
        )

    def mid_copies(half, t=0):
        rows = slice(t * W, (t + 1) * W) if half == 0 else rows_of(half)
        recv = hr if half else mr.at[t]
        return (
            to_row(mid.at[rows], mid_in.at[0, rows], ns.at[0], recv.at[0], 1),
            to_row(mid.at[rows], mid_in.at[1, rows], ns.at[1], recv.at[1], R - 1),
        )

    def start_rows(copies, before=()):
        for have, copy, old in zip((has_down, has_up), copies, before or (None, None)):

            @pl.when(have)
            def _():
                if old is not None:
                    old.wait_send()
                copy.start()

    def send_parts(half):
        rows = rows_of(half)
        part_out[0, rows] = acc1[rows, 0:CL].astype(BF16)
        part_out[1, rows] = acc1[rows, CL : 2 * CL].astype(BF16)
        start_rows(part_copies(half), (halo_down, halo_up) if half else ())

    def finish_mid(half):
        rows = rows_of(half)
        down, up = part_copies(half)

        @pl.when(has_up)
        def _():
            down.wait_recv()
            acc1[rows, 2 * CL :] += part_in[0, rows].astype(F32)

        @pl.when(has_down)
        def _():
            up.wait_recv()
            acc1[rows, 2 * CL :] += part_in[1, rows].astype(F32)

        mid[rows] = acc1[rows, 2 * CL :].astype(BF16)
        return local_stats(mid[rows].astype(F32))

    with jax.named_scope("parts of half 1"):
        z = place_other(3)
        last_latent_dots(z, 1, 0, 2 * CL)
        send_parts(1)
    with jax.named_scope("latent dots 3"):
        last_latent_dots(z, 0, 0, 2 * CL)
    with jax.named_scope("caches 3"):
        pass_on(cache_hop, 3)
    with jax.named_scope("cache dots 3"):
        z, _ = plane(3)
        place_caches(OWN + z - me)
        cache_dots(z, 0, 2 * CL)
        send_parts(0)
        last_latent_dots(z, 1, 2 * CL, 3 * CL)
        last_latent_dots(z, 0, 2 * CL, 3 * CL)
        cache_dots(z, 2 * CL, 3 * CL)
    with jax.named_scope("mid of half 1"):
        partial = finish_mid(1)
        start_rows(mid_copies(1), part_copies(1))

    with jax.named_scope("mid of half 0"):
        st2[0] = partial + finish_mid(0)
        wait_all(coef.at[pl.ds(1, Z - 1)], ss.at[0])
        share_stats(st2, ss.at[0], s2r.at[0])
        for t in range(2):
            start_rows(mid_copies(0, t))
        for hop in (latent_part(0), latent_part(1), cache_hop):
            for d in range(Z - 1):
                wait_sent(hop, d, last=True)
    with jax.named_scope("stats two"):
        coefs_two = (*finish_stats(st2, ss.at[0], s2r.at[0], gb[2:3, :]), gb[3:4, :])

    def place_mid(half, frames):
        down, up = mid_copies(half, frames[0] if half == 0 else 0)

        def place_row(dh, values):
            for t in frames:
                rows = slice(t * W, (t + 1) * W)
                there = slice(C2 + t * W, C2 + (t + 1) * W)
                put(xs2, there, dh * 3 * CL, normed(values[rows, :].astype(F32), coefs_two))

        place_row(1, mid)

        @pl.when(has_up)
        def _():
            down.wait_recv()
            place_row(0, mid_in.at[0])

        @pl.when(has_down)
        def _():
            up.wait_recv()
            place_row(2, mid_in.at[1])

    ZH = Z // 2
    mine = me // ZH

    def second_dots(frames, pair):
        cols = pl.ds(pl.multiple_of(pair * (ZH * CL), ZH * CL), ZH * CL)
        start, end = frames[0] * W, (frames[-1] + 1) * W
        for dt in (2, 1, 0):
            back = (2 - dt) * W
            low = max(start, back)
            if low >= end:
                continue
            term = jnp.dot(
                xs2[C2 + low - back : C2 + end - back, :], w2[dt, :, cols],
                preferred_element_type=F32,
            )
            for j in range(ZH):
                cut = term[:, j * CL : (j + 1) * CL]
                if start >= C2 and dt == 2:
                    acc2[pair * ZH + j, low:end] = cut
                else:
                    acc2[pair * ZH + j, low:end] += cut

    def frame(t):
        return slice(t * W, (t + 1) * W)

    def sum_copy(slot, half, k, to, rows=None):
        last = rows == frame(T - 1)
        rows = rows or rows_of(half)
        return to_chan(
            rs_out.at[k - 1, rows], rs_in.at[slot, rows],
            cs.at[half] if k == Z - 1 else ls.at[half, k - 1],
            rf.at[slot - 1] if last else rsr.at[half, slot], to,
        )

    def send_sum(half, k, slot, to, rows=None):
        whole = rows or rows_of(half)
        rs_out[k - 1, whole] = acc2[partner(k), whole].astype(BF16)
        if half == 1 and k < Z - 1:
            for t in (T - 2, T - 1):
                sum_copy(slot, half, k, to, frame(t)).start()
        else:
            sum_copy(slot, half, k, to, rows).start()

    MERGE = 0

    def send_merged(half):
        rows = rows_of(half)
        sum_copy(MERGE, half, 3, 1).wait_recv()
        rs_out[1, rows] = (acc2[partner(2), rows] + rs_in[MERGE, rows].astype(F32)).astype(BF16)
        if half == 0:
            sum_copy(2, half, 2, 2).start()
        else:
            for t in (T - 2, T - 1):
                sum_copy(2, half, 2, 2, frame(t)).start()

    def send_far(half, rows=None):
        @pl.when(edge)
        def _():
            send_sum(half, 3, MERGE, 1, rows)

        @pl.when(inner)
        def _():
            send_sum(half, 3, 3, 3, rows)

    near, far = mine, 1 - mine
    for t in range(T // 2):
        with jax.named_scope(f"place {t}"):
            place_mid(0, (t,))
        with jax.named_scope(f"conv2 far {t}"):
            second_dots((t,), far)
            send_far(0, slice(t * W, (t + 1) * W))

    @pl.when(edge)
    def _():
        send_sum(0, 2, 2, 2, slice(0, W))

    with jax.named_scope("place half 1"):
        place_mid(1, (2, 3))
    with jax.named_scope("conv2 half 1 far"):
        second_dots((2, 3), far)
        send_far(1)

        @pl.when(edge)
        def _():
            send_sum(0, 2, 2, 2, slice(W, 2 * W))

    with jax.named_scope("conv2 half 0 near"):
        second_dots((0, 1), near)

        @pl.when(edge)
        def _():
            send_sum(1, 2, 2, 2)

        @pl.when(inner)
        def _():
            send_sum(0, 1, 1, 1)

    with jax.named_scope("conv2 half 1 near"):
        second_dots((2, 3), near)

        @pl.when(inner)
        def _():
            send_sum(1, 1, 1, 1)

        lat_t[...] = lat_t[...] + acc2[me]
    with jax.named_scope("last sums out"):

        @pl.when(edge)
        def _():
            sum_copy(2, 0, 2, 2).wait_send()
            send_sum(0, 1, 1, 1)
            sum_copy(2, 1, 2, 2).wait_send()
            send_sum(1, 1, 1, 1)

        @pl.when(inner)
        def _():
            for half in range(2):
                send_merged(half)

    ei = lax.broadcasted_iota(jnp.int32, (W, 2 * W), 0)
    ej = lax.broadcasted_iota(jnp.int32, (W, 2 * W), 1) // 2
    twice = (ei == ej).astype(BF16)

    def finish_frame(t):
        rows = frame(t)
        total = lat_t[rows, :] + rs_in[1, rows].astype(F32) + rs_in[2, rows].astype(F32)
        wide = exact_dot(total.T, twice)
        for side in range(2):
            for again in range(2):
                out_ref[pl.ds(t * 4 + side * 2 + again, CL, stride=4 * T), :] = wide[
                    :, side * W : (side + 1) * W
                ]

    for half in range(2):

        @pl.when(inner)
        def _():
            rows = rows_of(half)
            sum_copy(3, half, 3, 3).wait_recv()
            lat_t[rows, :] += rs_in[3, rows].astype(F32)

    with jax.named_scope("sums wait 0"):
        sum_copy(1, 0, 1, 1).wait_recv()
        sum_copy(2, 0, 2, 2).wait_recv()
    with jax.named_scope("upsample 0"):
        finish_frame(0)
        finish_frame(1)
    for t in (T - 2, T - 1):
        with jax.named_scope(f"sums wait {t}"):
            sum_copy(1, 1, 1, 1, frame(t)).wait_recv()
            sum_copy(2, 1, 2, 2, frame(t)).wait_recv()
        with jax.named_scope(f"upsample {t}"):
            finish_frame(t)

    with jax.named_scope("sends wait"):
        for half in range(2):
            sum_copy(1, half, 3, 1).wait_send()
            sum_copy(1, half, 1, 1).wait_send()

        @pl.when(inner)
        def _():
            for half in range(2):
                sum_copy(2, half, 2, 2).wait_send()

        for have, way in ((has_down, 0), (has_up, 1)):

            @pl.when(have)
            def _():
                part_copies(0)[way].wait_send()
                wait_all(mid, ns.at[way])


def body(
    latents, cache_one, cache_two, gain_one, bias_one, weight_one, gain_two, bias_two, weight_two
):
    CL, T, rows_here, W = latents.shape
    R, Z = lax.axis_size("rows"), lax.axis_size("chan")
    if CL != 128 or W != 128 or rows_here != 1 or T != 4 or R < 2 or Z != 4:
        return plain_body(
            latents, cache_one, cache_two, gain_one, bias_one, weight_one, gain_two, bias_two,
            weight_two,
        )
    C = CL * Z
    M = T * W
    hbm = pl.BlockSpec(memory_space=pltpu.HBM)
    dma = pltpu.SemaphoreType.DMA
    out = pl.pallas_call(
        functools.partial(block_kernel, R, Z, CL, T, W),
        out_shape=jax.ShapeDtypeStruct((CL * T * 4, W), F32),
        in_specs=[hbm] * 9,
        out_specs=pl.BlockSpec(memory_space=pltpu.VMEM),
        scratch_shapes=[
            pltpu.VMEM((CL * T, W), BF16),
            pltpu.VMEM((2, CL * 2, W), BF16),
            pltpu.VMEM((8, CL), F32),
            pltpu.VMEM((CL * T, W), F32),
            pltpu.VMEM((M, CL), F32),
            pltpu.VMEM((2 * Z - 1, CL * T, W), BF16),
            pltpu.VMEM((2 * Z - 1, 2 * W, CL), BF16),
            pltpu.VMEM((M, 3 * CL), BF16),
            pltpu.VMEM((2 * W, 3 * CL), BF16),
            pltpu.VMEM((M, 3 * CL), F32),
            pltpu.VMEM((2, M, CL), BF16),
            pltpu.VMEM((2, M, CL), BF16),
            pltpu.VMEM((M, CL), BF16),
            pltpu.VMEM((2, M, CL), BF16),
            pltpu.VMEM((3, 2 * W, CL), BF16),
            pltpu.VMEM((M + 2 * W, 9 * CL), BF16),
            pltpu.VMEM((Z, M, CL), F32),
            pltpu.VMEM((R, 8, CL), F32),
            pltpu.VMEM((R, 8, CL), F32),
            pltpu.VMEM((Z, 8, CL), F32),
            pltpu.VMEM((Z - 1, M, CL), BF16),
            pltpu.VMEM((Z, M, CL), BF16),
            pltpu.VMEM((3, 3, C, 3 * CL), BF16),
            pltpu.VMEM((3, 9 * CL, C), BF16),
            dma((3,)), dma((2,)),
            dma((2, 2)), dma((2, 2, 2)), dma((2,)),
            dma((2,)), dma((2, Z - 1)),
            dma((1,)), dma((1,)), dma((1,)), dma((1,)),
            dma((4,)), dma((2,)), dma((2, 2)), dma((2, 2)),
            dma((2, Z)), dma((2,)),
        ],
        compiler_params=pltpu.CompilerParams(
            collective_id=0, has_side_effects=True, vmem_limit_bytes=40 * 1024 * 1024
        ),
    )(*(pltpu.with_memory_space_constraint(v, pltpu.HBM) for v in (
        latents.reshape(CL * T, W),
        cache_one.reshape(CL * 2, W),
        cache_two.reshape(CL * 2, W),
        gain_one.reshape(1, CL),
        bias_one.reshape(1, CL),
        gain_two.reshape(1, CL),
        bias_two.reshape(1, CL),
        weight_one,
        weight_two.reshape(3, 9 * CL, C),
    )))
    return out.reshape(CL, T, 2, 2, W).transpose(0, 1, 3, 2, 4).reshape(CL, T, 2, 2 * W)


def solution(mesh):
    return jax.shard_map(
        body,
        mesh=mesh,
        in_specs=(
            P("chan", None, "rows", None),
            P("chan", None, "rows", None),
            P("chan", None, "rows", None),
            P("chan"),
            P("chan"),
            P(None, None, None, None, "chan"),
            P("chan"),
            P("chan"),
            P(None, None, None, "chan", None),
        ),
        out_specs=P("chan", None, "rows", None),
        check_vma=False,
    )
```

```python
import functools

import jax
import jax.numpy as jnp
from jax import lax
from jax.experimental import pallas as pl
from jax.experimental.pallas import tpu as pltpu
from jax.sharding import PartitionSpec as P

CHANNELS = 512
GROUPS = 32
MESH = pl.DeviceIdType.MESH
F32 = jnp.float32
BF16 = jnp.bfloat16


epsilon = 1e-06


def padded(block, sides, width):
    for axis, dim in sides:
        count = lax.axis_size(axis)
        forward = [(i, i + 1) for i in range(count - 1)]
        backward = [(target, source) for source, target in forward]
        low = lax.ppermute(
            lax.slice_in_dim(block, block.shape[dim] - width, None, axis=dim), axis, forward
        )
        high = lax.ppermute(lax.slice_in_dim(block, 0, width, axis=dim), axis, backward)
        block = jnp.concatenate([low, block, high], axis=dim)
    return block


def group_silu(values, gain, bias):
    group_size = CHANNELS // GROUPS
    grouped = values.reshape(values.shape[0] // group_size, -1)
    sums, squares = lax.psum((jnp.sum(grouped, axis=1), jnp.sum(grouped * grouped, axis=1)), "rows")
    members = grouped.shape[1] * lax.axis_size("rows")
    average = sums / members
    spread = squares / members - average * average
    normed = ((grouped - average[:, None]) * lax.rsqrt(spread + epsilon)[:, None]).reshape(
        values.shape
    )
    scaled = normed * gain[:, None, None, None] + bias[:, None, None, None]
    return jax.nn.silu(scaled).astype(jnp.bfloat16)


def pad_rows(frames):
    return padded(frames, (("rows", 2),), 1)


def conv_block(frames, kernel):
    result = lax.conv_general_dilated(
        frames[None],
        kernel,
        (1, 1, 1),
        ((0, 0), (0, 0), (1, 1)),
        dimension_numbers=("NCDHW", "DHWIO", "NCDHW"),
        preferred_element_type=jnp.float32,
    )
    return result[0]


def gathered_conv(frames, kernel):
    channels = lax.all_gather(frames, "chan", axis=0, tiled=True)
    return conv_block(channels, kernel)


def plain_body(
    latents, cache_one, cache_two, gain_one, bias_one, weight_one, gain_two, bias_two, weight_two
):
    floats = latents.astype(jnp.float32)
    first = group_silu(floats, gain_one, bias_one)
    frames_one = pad_rows(jnp.concatenate([cache_one, first], axis=1))
    middle = gathered_conv(frames_one, weight_one).astype(jnp.bfloat16)
    second = group_silu(middle.astype(jnp.float32), gain_two, bias_two)
    frames_two = pad_rows(jnp.concatenate([cache_two, second], axis=1))
    columns = lax.all_to_all(weight_two, "chan", split_axis=4, concat_axis=3, tiled=True)
    result = floats + gathered_conv(frames_two, columns)
    return jnp.repeat(jnp.repeat(result, 2, axis=2), 2, axis=3)


def block_kernel(
    R, Z, CL, T, W,
    lat_hbm, c1_hbm, c2_hbm, g1_hbm, b1_hbm, g2_hbm, b2_hbm, w1_hbm, w2_hbm,
    out_ref,
    lat_v, c_v, gb,
    tmp, lat_t, raw, xc, xs1, xsc, acc1, part_out, part_in, mid, mid_in, x2, xs2, acc2,
    st1, st2, coef, rs_out, rs_in, w1, w2,
    isem, wsem, ls, lr, lr3, cs, cr, ss, kr, s1r, s2r, ns, hr, pr, mr, rsr, rf,
):
    row = lax.axis_index("rows")
    me = lax.axis_index("chan")
    M = T * W
    C2 = 2 * W
    H = M // 2
    HL = CL * T // 2
    OWN = Z - 1
    has_up = row > 0
    has_down = row < R - 1
    edge = jnp.logical_or(me == 0, me == Z - 1)
    inner = jnp.logical_not(edge)
    is_inner = ((me + 1) // 2) % 2

    def partner(k):
        other = me * 0
        bit = 1
        while bit < Z:
            mine = (me // bit) % 2
            other = other + bit * ((1 - mine) if k & bit else mine)
            bit *= 2
        return other

    st1[...] = jnp.zeros_like(st1)
    st2[...] = jnp.zeros_like(st2)
    barrier = pltpu.get_barrier_semaphore()
    for k in range(1, R):
        pl.semaphore_signal(barrier, inc=1, device_id={"rows": lax.rem(row + k, R)}, device_id_type=MESH)
    for k in range(1, Z):
        pl.semaphore_signal(barrier, inc=1, device_id={"chan": partner(k)}, device_id_type=MESH)

    lat_load = pltpu.make_async_copy(lat_hbm, lat_v, isem.at[0])
    loads = [
        lat_load,
        pltpu.make_async_copy(c1_hbm, c_v.at[0], isem.at[1]),
        pltpu.make_async_copy(c2_hbm, c_v.at[1], isem.at[1]),
    ] + [
        pltpu.make_async_copy(v, gb.at[pl.ds(i, 1)], isem.at[2])
        for i, v in enumerate((g1_hbm, b1_hbm, g2_hbm, b2_hbm))
    ]
    place = (0, 2, 1)
    w_copies = []
    for dt in range(3):
        for dh in range(3):
            w_copies.append(
                pltpu.make_async_copy(
                    w1_hbm.at[dt, dh],
                    w1.at[dt, :, :, pl.ds(place[dh] * CL, CL)],
                    wsem.at[0],
                )
            )
    w2_copy = pltpu.make_async_copy(w2_hbm, w2, wsem.at[1])
    for copy in loads:
        copy.start()

    def wait_all(whole, sem):
        pltpu.make_async_copy(whole, whole, sem).wait()

    def to_chan(src, dst, send, recv, k):
        return pltpu.make_async_remote_copy(
            src_ref=src, dst_ref=dst, send_sem=send, recv_sem=recv,
            device_id={"chan": partner(k)}, device_id_type=MESH,
        )

    def to_row(src, dst, send, recv, k):
        return pltpu.make_async_remote_copy(
            src_ref=src, dst_ref=dst, send_sem=send, recv_sem=recv,
            device_id={"rows": lax.rem(row + k, R)}, device_id_type=MESH,
        )

    def along(src, buffer, send, recv, d, part, side):
        slot = OWN - side * d
        return pltpu.make_async_remote_copy(
            src_ref=src, dst_ref=buffer.at[(slot - side, *part)],
            send_sem=send, recv_sem=recv,
            device_id={"chan": me + side}, device_id_type=MESH,
        )

    def latent_hop(d, ch, side):
        slot = OWN - side * d
        rows = pl.ds(ch * HL, HL)
        src = lat_hbm.at[rows] if d == 0 else raw.at[slot, rows]
        way = (side + 1) // 2
        arrival = lr.at[way, d, ch] if d < 2 else lr3.at[way]
        return along(
            src, raw, ls.at[(side + 1) // 2, ch], arrival, d, (rows,), side
        )

    def cache_hop(d, side):
        slot = OWN - side * d
        return along(
            xc.at[slot], xc, cs.at[(side + 1) // 2], cr.at[(side + 1) // 2, d], d, (), side
        )

    def arrives(d, side):
        return me >= d if side > 0 else me + d <= Z - 1

    def goes(d, side):
        return jnp.logical_and(arrives(d, side), me < Z - 1 if side > 0 else me > 0)

    def also(here, some):
        return here if some is None else jnp.logical_and(here, some)

    def start_hop(hop, d, some=None):
        for side in (1, -1):

            @pl.when(also(goes(d, side), some))
            def _():
                if d > 0:
                    hop(d - 1, side).wait_send()
                hop(d, side).start()

    def wait_hop(hop, d, some=None):
        for side in (1, -1):

            @pl.when(also(arrives(d, side), some))
            def _():
                hop(d - 1, side).wait_recv()

    def wait_sent(hop, d, last=False):
        for side in (1, -1):
            here = goes(d, side)
            if last and d < Z - 2:
                here = jnp.logical_and(here, jnp.logical_not(goes(d + 1, side)))

            @pl.when(here)
            def _():
                hop(d, side).wait_send()

    def pass_on(hop, d, some=None):
        wait_hop(hop, d, some)
        if d < Z - 1:
            start_hop(hop, d, some)

    def latent_part(ch):
        return lambda d, side: latent_hop(d, ch, side)

    members = F32(R * M * (CHANNELS // GROUPS))
    gi = lax.broadcasted_iota(jnp.int32, (CL, CL), 0) // (CHANNELS // GROUPS)
    gj = lax.broadcasted_iota(jnp.int32, (CL, CL), 1) // (CHANNELS // GROUPS)
    same_group = (gi == gj).astype(BF16)

    def exact_dot(values, ones):
        terms = []
        for _ in range(3):
            terms.append(values.astype(BF16))
            values = values - terms[-1].astype(F32)
        count = terms[0].shape[0]
        out = jnp.dot(jnp.concatenate(terms, axis=0), ones, preferred_element_type=F32)
        return out[0:count] + out[count : 2 * count] + out[2 * count :]

    which = lax.broadcasted_iota(jnp.int32, (8, CL), 0)

    def local_stats(values):
        sums = jnp.sum(values, axis=0, keepdims=True)
        squares = jnp.sum(values * values, axis=0, keepdims=True)
        return jnp.where(which == 0, sums, jnp.where(which == 1, squares, 0.0))

    def share_stats(st, send, recv):
        for k in range(1, R):
            to_row(st.at[0, pl.ds(0, 2)], st.at[k, pl.ds(0, 2)], send, recv, k).start()

    def finish_stats(st, send, recv, gain):
        wait_all(st.at[pl.ds(1, R - 1), pl.ds(0, 2)], recv)
        wait_all(st.at[pl.ds(1, R - 1), pl.ds(0, 2)], send)
        total = st[0]
        for k in range(1, R):
            total = total + st[k]
        total = exact_dot(total, same_group) / members
        mean = total[0:1, :]
        spread = jnp.maximum(total[1:2, :] - mean * mean, 0.0)
        return mean, lax.rsqrt(spread + epsilon) * gain

    def normed(values, coefs):
        mean, scale, bias = coefs
        u = (values - mean) * scale + bias
        return (u / (1.0 + jnp.exp(-u))).astype(BF16)

    def shifted(block):
        rows = block.shape[0]
        cell = lax.broadcasted_iota(jnp.int32, (rows, CL), 0) % W
        wide = block.astype(F32)
        left = jnp.where(cell == 0, 0.0, pltpu.roll(wide, 1, 0)).astype(BF16)
        right = jnp.where(cell == W - 1, 0.0, pltpu.roll(wide, rows - 1, 0)).astype(BF16)
        return left, block, right

    def put(dst, rows, column, block):
        for dx, value in enumerate(shifted(block)):
            dst[rows, column + dx * CL : column + (dx + 1) * CL] = value

    with jax.named_scope("barrier wait"):
        pl.semaphore_wait(barrier, R - 1 + Z - 1)

    start_hop(latent_part(0), 0)
    for copy in w_copies:
        copy.start()

    halo_down = to_row(x2.at[1], x2.at[0], ns.at[0], hr.at[0], 1)
    halo_up = to_row(x2.at[1], x2.at[2], ns.at[1], hr.at[1], R - 1)

    with jax.named_scope("own latents"):
        lat_load.wait()
        tmp[...] = lat_v[...].astype(F32)
        for t in range(T):
            lat_t[t * W : (t + 1) * W, :] = tmp[pl.ds(t, CL, stride=T), :].T
        st1[0] = local_stats(lat_t[...])
        share_stats(st1, ss.at[0], s1r.at[0])

    with jax.named_scope("own caches"):
        wait_all(c_v, isem.at[1])
        for i, (buffer, slot) in enumerate(((xc, OWN), (x2, 1))):
            tmp[0 : 2 * CL, :] = c_v[i].astype(F32)
            for t in range(2):
                buffer[slot, t * W : (t + 1) * W, :] = (
                    tmp[pl.ds(t, CL, stride=2), :].T.astype(BF16)
                )
        acc1[...] = jnp.zeros_like(acc1)

    start_hop(latent_part(1), 0)

    @pl.when(has_down)
    def _():
        halo_down.start()

    @pl.when(has_up)
    def _():
        halo_up.start()

    def kernel_one(dt, z, low, high):
        base = pl.ds(pl.multiple_of(z * CL, CL), CL)
        return jnp.concatenate([w1[dt, dx, base, low:high] for dx in range(3)], axis=0)

    def latent_dots(z):
        for dt in (2, 1, 0):
            start = (2 - dt) * W
            acc1[start:, :] += jnp.dot(
                xs1[0 : M - start, :], kernel_one(dt, z, 0, 3 * CL), preferred_element_type=F32
            )

    def last_latent_dots(z, half, low, high):
        for dt in (2, 1, 0):
            first = half * H - (2 - dt) * W
            skip = max(0, -first)
            if skip < H:
                acc1[half * H + skip : (half + 1) * H, low:high] += jnp.dot(
                    xs1[first + skip : first + H, :], kernel_one(dt, z, low, high),
                    preferred_element_type=F32,
                )

    def cache_dots(z, low, high):
        for dt in range(2):
            acc1[0 : C2 - dt * W, low:high] += jnp.dot(
                xsc[dt * W : C2, :], kernel_one(dt, z, low, high), preferred_element_type=F32
            )

    def place_caches(slot):
        for t in range(2):
            rows = slice(t * W, (t + 1) * W)
            put(xsc, rows, 0, xc[slot, rows, :])

    def place_latents(slot, coefs):
        tmp[...] = raw[slot].astype(F32)
        for t in range(T):
            put(
                xs1, slice(t * W, (t + 1) * W), 0,
                normed(tmp[pl.ds(t, CL, stride=T), :].T, coefs),
            )

    def plane(k):
        if k == 1:
            return partner(1), 1
        a, b = partner(2), partner(3)
        if k == 2:
            return a + is_inner * (b - a), 2 + is_inner
        return b + is_inner * (a - b), 3 - is_inner

    def place_other(k):
        z, at = plane(k)
        place_latents(OWN + z - me, tuple(coef[at, i : i + 1, :] for i in range(3)))
        return z

    def other_latents(k):
        latent_dots(place_other(k))

    wait_all(w1, wsem.at[0])
    w2_copy.start()
    with jax.named_scope("own cache dots"):
        place_caches(OWN)
        cache_dots(me, 0, 3 * CL)
    start_hop(cache_hop, 0)

    with jax.named_scope("stats one"):
        wait_all(gb.at[pl.ds(0, 4)], isem.at[2])
        mean, scale = finish_stats(st1, ss.at[0], s1r.at[0], gb[0:1, :])
        bias = gb[1:2, :]
        coef[0] = jnp.where(which == 0, mean, jnp.where(which == 1, scale, bias))
        for k in range(1, Z):
            to_chan(coef.at[0], coef.at[k], ss.at[0], kr.at[0], k).start()

    with jax.named_scope("latents 1, part 0"):
        pass_on(latent_part(0), 1)

    with jax.named_scope("own latent dots"):
        for t in range(T):
            rows = slice(t * W, (t + 1) * W)
            put(xs1, rows, 0, normed(lat_t[rows, :], (mean, scale, bias)))
        latent_dots(me)
    with jax.named_scope("latents 1, part 1"):
        pass_on(latent_part(1), 1)
    with jax.named_scope("conv2 of caches"):
        w2_copy.wait()

        @pl.when(has_up)
        def _():
            halo_down.wait_recv()

        @pl.when(has_down)
        def _():
            halo_up.wait_recv()

        @pl.when(jnp.logical_not(has_up))
        def _():
            x2[0] = jnp.zeros((C2, CL), BF16)
            xs2[C2:, 0 : 3 * CL] = jnp.zeros((M, 3 * CL), BF16)

        @pl.when(jnp.logical_not(has_down))
        def _():
            x2[2] = jnp.zeros((C2, CL), BF16)
            xs2[C2:, 6 * CL :] = jnp.zeros((M, 3 * CL), BF16)

        for dh in range(3):
            put(xs2, slice(0, C2), dh * 3 * CL, x2[dh])
        both = jnp.dot(xs2[0:C2, :], w2[0], preferred_element_type=F32)
        one = jnp.dot(xs2[W:C2, :], w2[1], preferred_element_type=F32)
        for d in range(Z):
            cols = slice(d * CL, (d + 1) * CL)
            acc2[d, 0:W] = both[0:W, cols] + one[:, cols]
            acc2[d, W:C2] = both[W:C2, cols]
    with jax.named_scope("caches 1"):
        pass_on(cache_hop, 1)
    with jax.named_scope("latents 2, part 0"):
        pass_on(latent_part(0), 2)
    with jax.named_scope("latent dots 1"):
        wait_all(coef.at[pl.ds(1, Z - 1)], kr.at[0])
        other_latents(1)
    with jax.named_scope("latents 2, part 1"):
        pass_on(latent_part(1), 2)
    with jax.named_scope("latent dots 2"):
        other_latents(2)
    with jax.named_scope("caches 2"):
        pass_on(cache_hop, 2)
    with jax.named_scope("cache dots 1"):
        z, _ = plane(1)
        place_caches(OWN + z - me)
        cache_dots(z, 0, 3 * CL)
    with jax.named_scope("cache dots 2"):
        z, _ = plane(2)
        place_caches(OWN + z - me)
        cache_dots(z, 0, 3 * CL)

    with jax.named_scope("latents 3"):
        for side in (1, -1):

            @pl.when(arrives(Z - 1, side))
            def _():
                wait_all(raw.at[OWN - side * (Z - 1)], lr3.at[(side + 1) // 2])

    def rows_of(half):
        return slice(half * H, (half + 1) * H)

    def part_copies(half):
        rows = rows_of(half)
        return (
            to_row(part_out.at[0, rows], part_in.at[0, rows], ns.at[2 - 2 * half], pr.at[0, half], 1),
            to_row(part_out.at[1, rows], part_in.at[1, rows], ns.at[3 - 2 * half], pr.at[1, half], R - 1),
        )

    def mid_copies(half, t=0):
        rows = slice(t * W, (t + 1) * W) if half == 0 else rows_of(half)
        recv = hr if half else mr.at[t]
        return (
            to_row(mid.at[rows], mid_in.at[0, rows], ns.at[0], recv.at[0], 1),
            to_row(mid.at[rows], mid_in.at[1, rows], ns.at[1], recv.at[1], R - 1),
        )

    def start_rows(copies, before=()):
        for have, copy, old in zip((has_down, has_up), copies, before or (None, None)):

            @pl.when(have)
            def _():
                if old is not None:
                    old.wait_send()
                copy.start()

    def send_parts(half):
        rows = rows_of(half)
        part_out[0, rows] = acc1[rows, 0:CL].astype(BF16)
        part_out[1, rows] = acc1[rows, CL : 2 * CL].astype(BF16)
        start_rows(part_copies(half), (halo_down, halo_up) if half else ())

    def finish_mid(half):
        rows = rows_of(half)
        down, up = part_copies(half)

        @pl.when(has_up)
        def _():
            down.wait_recv()
            acc1[rows, 2 * CL :] += part_in[0, rows].astype(F32)

        @pl.when(has_down)
        def _():
            up.wait_recv()
            acc1[rows, 2 * CL :] += part_in[1, rows].astype(F32)

        mid[rows] = acc1[rows, 2 * CL :].astype(BF16)
        return local_stats(mid[rows].astype(F32))

    with jax.named_scope("parts of half 1"):
        z = place_other(3)
        last_latent_dots(z, 1, 0, 2 * CL)
        send_parts(1)
    with jax.named_scope("latent dots 3"):
        last_latent_dots(z, 0, 0, 2 * CL)
    with jax.named_scope("caches 3"):
        pass_on(cache_hop, 3)
    with jax.named_scope("cache dots 3"):
        z, _ = plane(3)
        place_caches(OWN + z - me)
        cache_dots(z, 0, 2 * CL)
        send_parts(0)
        last_latent_dots(z, 1, 2 * CL, 3 * CL)
        last_latent_dots(z, 0, 2 * CL, 3 * CL)
        cache_dots(z, 2 * CL, 3 * CL)
    with jax.named_scope("mid of half 1"):
        partial = finish_mid(1)
        start_rows(mid_copies(1), part_copies(1))

    with jax.named_scope("mid of half 0"):
        st2[0] = partial + finish_mid(0)
        wait_all(coef.at[pl.ds(1, Z - 1)], ss.at[0])
        share_stats(st2, ss.at[0], s2r.at[0])
        for t in range(2):
            start_rows(mid_copies(0, t))
        for hop in (latent_part(0), latent_part(1), cache_hop):
            for d in range(Z - 1):
                wait_sent(hop, d, last=True)
    with jax.named_scope("stats two"):
        coefs_two = (*finish_stats(st2, ss.at[0], s2r.at[0], gb[2:3, :]), gb[3:4, :])

    def place_mid(half, frames):
        down, up = mid_copies(half, frames[0] if half == 0 else 0)

        def place_row(dh, values):
            for t in frames:
                rows = slice(t * W, (t + 1) * W)
                there = slice(C2 + t * W, C2 + (t + 1) * W)
                put(xs2, there, dh * 3 * CL, normed(values[rows, :].astype(F32), coefs_two))

        place_row(1, mid)

        @pl.when(has_up)
        def _():
            down.wait_recv()
            place_row(0, mid_in.at[0])

        @pl.when(has_down)
        def _():
            up.wait_recv()
            place_row(2, mid_in.at[1])

    ZH = Z // 2
    mine = me // ZH

    def second_dots(frames, pair):
        cols = pl.ds(pl.multiple_of(pair * (ZH * CL), ZH * CL), ZH * CL)
        start, end = frames[0] * W, (frames[-1] + 1) * W
        for dt in (2, 1, 0):
            back = (2 - dt) * W
            low = max(start, back)
            if low >= end:
                continue
            term = jnp.dot(
                xs2[C2 + low - back : C2 + end - back, :], w2[dt, :, cols],
                preferred_element_type=F32,
            )
            for j in range(ZH):
                cut = term[:, j * CL : (j + 1) * CL]
                if start >= C2 and dt == 2:
                    acc2[pair * ZH + j, low:end] = cut
                else:
                    acc2[pair * ZH + j, low:end] += cut

    def frame(t):
        return slice(t * W, (t + 1) * W)

    def sum_copy(slot, half, k, to, rows=None):
        last = rows == frame(T - 1)
        rows = rows or rows_of(half)
        return to_chan(
            rs_out.at[k - 1, rows], rs_in.at[slot, rows],
            cs.at[half] if k == Z - 1 else ls.at[half, k - 1],
            rf.at[slot] if last and slot < Z - 1 else rsr.at[half, slot], to,
        )

    def send_sum(half, k, slot, to, rows=None):
        whole = rows or rows_of(half)
        rs_out[k - 1, whole] = acc2[partner(k), whole].astype(BF16)
        if half == 1 and k < Z - 1:
            for t in (T - 2, T - 1):
                sum_copy(slot, half, k, to, frame(t)).start()
        else:
            sum_copy(slot, half, k, to, rows).start()

    MERGE = 0

    def send_merged(half):
        for rows in (rows_of(0),) if half == 0 else (frame(T - 2), frame(T - 1)):
            sum_copy(MERGE, half, 3, 1, rows).wait_recv()
            rs_out[1, rows] = (acc2[partner(2), rows] + rs_in[MERGE, rows].astype(F32)).astype(BF16)
            sum_copy(2, half, 2, 2, rows).start()

    def send_far(half, rows=None):
        @pl.when(edge)
        def _():
            send_sum(half, 3, MERGE, 1, rows)

        @pl.when(inner)
        def _():
            send_sum(half, 3, 3, 3, rows)

    near, far = mine, 1 - mine
    for t in range(T // 2):
        with jax.named_scope(f"place {t}"):
            place_mid(0, (t,))
        with jax.named_scope(f"conv2 far {t}"):
            second_dots((t,), far)
            send_far(0, slice(t * W, (t + 1) * W))

    with jax.named_scope("place half 1"):
        place_mid(1, (2, 3))
    with jax.named_scope("conv2 half 1 far"):
        for t in (T - 2, T - 1):
            second_dots((t,), far)
            send_far(1, frame(t))

    with jax.named_scope("conv2 half 0 near"):
        second_dots((0, 1), near)
        send_sum(0, 1, 1, 1)

    with jax.named_scope("conv2 half 1 near"):
        second_dots((2, 3), near)
        send_sum(1, 1, 1, 1)
        lat_t[...] = lat_t[...] + acc2[me]
    with jax.named_scope("last sums out"):

        @pl.when(edge)
        def _():
            for half in range(2):
                sum_copy(1, half, 1, 1).wait_send()
                send_sum(half, 2, 2, 2)

        @pl.when(inner)
        def _():
            for half in range(2):
                send_merged(half)

    ei = lax.broadcasted_iota(jnp.int32, (W, 2 * W), 0)
    ej = lax.broadcasted_iota(jnp.int32, (W, 2 * W), 1) // 2
    twice = (ei == ej).astype(BF16)

    def finish_frame(t):
        rows = frame(t)
        total = lat_t[rows, :] + rs_in[1, rows].astype(F32) + rs_in[2, rows].astype(F32)
        wide = exact_dot(total.T, twice)
        for side in range(2):
            for again in range(2):
                out_ref[pl.ds(t * 4 + side * 2 + again, CL, stride=4 * T), :] = wide[
                    :, side * W : (side + 1) * W
                ]

    for half in range(2):

        @pl.when(inner)
        def _():
            rows = rows_of(half)
            sum_copy(3, half, 3, 3).wait_recv()
            lat_t[rows, :] += rs_in[3, rows].astype(F32)

    with jax.named_scope("sums wait 0"):
        sum_copy(1, 0, 1, 1).wait_recv()
        sum_copy(2, 0, 2, 2).wait_recv()
    with jax.named_scope("upsample 0"):
        finish_frame(0)
        finish_frame(1)
    for t in (T - 2, T - 1):
        with jax.named_scope(f"sums wait {t}"):
            sum_copy(1, 1, 1, 1, frame(t)).wait_recv()
            sum_copy(2, 1, 2, 2, frame(t)).wait_recv()
        with jax.named_scope(f"upsample {t}"):
            finish_frame(t)

    with jax.named_scope("sends wait"):
        for half in range(2):
            sum_copy(1, half, 3, 1).wait_send()
            sum_copy(2, half, 2, 2).wait_send()

            @pl.when(inner)
            def _():
                sum_copy(1, half, 1, 1).wait_send()

        for have, way in ((has_down, 0), (has_up, 1)):

            @pl.when(have)
            def _():
                part_copies(0)[way].wait_send()
                wait_all(mid, ns.at[way])


def body(
    latents, cache_one, cache_two, gain_one, bias_one, weight_one, gain_two, bias_two, weight_two
):
    CL, T, rows_here, W = latents.shape
    R, Z = lax.axis_size("rows"), lax.axis_size("chan")
    if CL != 128 or W != 128 or rows_here != 1 or T != 4 or R < 2 or Z != 4:
        return plain_body(
            latents, cache_one, cache_two, gain_one, bias_one, weight_one, gain_two, bias_two,
            weight_two,
        )
    C = CL * Z
    M = T * W
    hbm = pl.BlockSpec(memory_space=pltpu.HBM)
    dma = pltpu.SemaphoreType.DMA
    out = pl.pallas_call(
        functools.partial(block_kernel, R, Z, CL, T, W),
        out_shape=jax.ShapeDtypeStruct((CL * T * 4, W), F32),
        in_specs=[hbm] * 9,
        out_specs=pl.BlockSpec(memory_space=pltpu.VMEM),
        scratch_shapes=[
            pltpu.VMEM((CL * T, W), BF16),
            pltpu.VMEM((2, CL * 2, W), BF16),
            pltpu.VMEM((8, CL), F32),
            pltpu.VMEM((CL * T, W), F32),
            pltpu.VMEM((M, CL), F32),
            pltpu.VMEM((2 * Z - 1, CL * T, W), BF16),
            pltpu.VMEM((2 * Z - 1, 2 * W, CL), BF16),
            pltpu.VMEM((M, 3 * CL), BF16),
            pltpu.VMEM((2 * W, 3 * CL), BF16),
            pltpu.VMEM((M, 3 * CL), F32),
            pltpu.VMEM((2, M, CL), BF16),
            pltpu.VMEM((2, M, CL), BF16),
            pltpu.VMEM((M, CL), BF16),
            pltpu.VMEM((2, M, CL), BF16),
            pltpu.VMEM((3, 2 * W, CL), BF16),
            pltpu.VMEM((M + 2 * W, 9 * CL), BF16),
            pltpu.VMEM((Z, M, CL), F32),
            pltpu.VMEM((R, 8, CL), F32),
            pltpu.VMEM((R, 8, CL), F32),
            pltpu.VMEM((Z, 8, CL), F32),
            pltpu.VMEM((Z - 1, M, CL), BF16),
            pltpu.VMEM((Z, M, CL), BF16),
            pltpu.VMEM((3, 3, C, 3 * CL), BF16),
            pltpu.VMEM((3, 9 * CL, C), BF16),
            dma((3,)), dma((2,)),
            dma((2, 2)), dma((2, 2, 2)), dma((2,)),
            dma((2,)), dma((2, Z - 1)),
            dma((1,)), dma((1,)), dma((1,)), dma((1,)),
            dma((4,)), dma((2,)), dma((2, 2)), dma((2, 2)),
            dma((2, Z)), dma((3,)),
        ],
        compiler_params=pltpu.CompilerParams(
            collective_id=0, has_side_effects=True, vmem_limit_bytes=40 * 1024 * 1024
        ),
    )(*(pltpu.with_memory_space_constraint(v, pltpu.HBM) for v in (
        latents.reshape(CL * T, W),
        cache_one.reshape(CL * 2, W),
        cache_two.reshape(CL * 2, W),
        gain_one.reshape(1, CL),
        bias_one.reshape(1, CL),
        gain_two.reshape(1, CL),
        bias_two.reshape(1, CL),
        weight_one,
        weight_two.reshape(3, 9 * CL, C),
    )))
    return out.reshape(CL, T, 2, 2, W).transpose(0, 1, 3, 2, 4).reshape(CL, T, 2, 2 * W)


def solution(mesh):
    return jax.shard_map(
        body,
        mesh=mesh,
        in_specs=(
            P("chan", None, "rows", None),
            P("chan", None, "rows", None),
            P("chan", None, "rows", None),
            P("chan"),
            P("chan"),
            P(None, None, None, None, "chan"),
            P("chan"),
            P("chan"),
            P(None, None, None, "chan", None),
        ),
        out_specs=P("chan", None, "rows", None),
        check_vma=False,
    )
```

```python
import functools

import jax
import jax.numpy as jnp
from jax import lax
from jax.experimental import pallas as pl
from jax.experimental.pallas import tpu as pltpu
from jax.sharding import PartitionSpec as P

CHANNELS = 512
GROUPS = 32
MESH = pl.DeviceIdType.MESH
F32 = jnp.float32
BF16 = jnp.bfloat16


epsilon = 1e-06


def padded(block, sides, width):
    for axis, dim in sides:
        count = lax.axis_size(axis)
        forward = [(i, i + 1) for i in range(count - 1)]
        backward = [(target, source) for source, target in forward]
        low = lax.ppermute(
            lax.slice_in_dim(block, block.shape[dim] - width, None, axis=dim), axis, forward
        )
        high = lax.ppermute(lax.slice_in_dim(block, 0, width, axis=dim), axis, backward)
        block = jnp.concatenate([low, block, high], axis=dim)
    return block


def group_silu(values, gain, bias):
    group_size = CHANNELS // GROUPS
    grouped = values.reshape(values.shape[0] // group_size, -1)
    sums, squares = lax.psum((jnp.sum(grouped, axis=1), jnp.sum(grouped * grouped, axis=1)), "rows")
    members = grouped.shape[1] * lax.axis_size("rows")
    average = sums / members
    spread = squares / members - average * average
    normed = ((grouped - average[:, None]) * lax.rsqrt(spread + epsilon)[:, None]).reshape(
        values.shape
    )
    scaled = normed * gain[:, None, None, None] + bias[:, None, None, None]
    return jax.nn.silu(scaled).astype(jnp.bfloat16)


def pad_rows(frames):
    return padded(frames, (("rows", 2),), 1)


def conv_block(frames, kernel):
    result = lax.conv_general_dilated(
        frames[None],
        kernel,
        (1, 1, 1),
        ((0, 0), (0, 0), (1, 1)),
        dimension_numbers=("NCDHW", "DHWIO", "NCDHW"),
        preferred_element_type=jnp.float32,
    )
    return result[0]


def gathered_conv(frames, kernel):
    channels = lax.all_gather(frames, "chan", axis=0, tiled=True)
    return conv_block(channels, kernel)


def plain_body(
    latents, cache_one, cache_two, gain_one, bias_one, weight_one, gain_two, bias_two, weight_two
):
    floats = latents.astype(jnp.float32)
    first = group_silu(floats, gain_one, bias_one)
    frames_one = pad_rows(jnp.concatenate([cache_one, first], axis=1))
    middle = gathered_conv(frames_one, weight_one).astype(jnp.bfloat16)
    second = group_silu(middle.astype(jnp.float32), gain_two, bias_two)
    frames_two = pad_rows(jnp.concatenate([cache_two, second], axis=1))
    columns = lax.all_to_all(weight_two, "chan", split_axis=4, concat_axis=3, tiled=True)
    result = floats + gathered_conv(frames_two, columns)
    return jnp.repeat(jnp.repeat(result, 2, axis=2), 2, axis=3)


def block_kernel(
    R, Z, CL, T, W,
    lat_hbm, c1_hbm, c2_hbm, g1_hbm, b1_hbm, g2_hbm, b2_hbm, w1_hbm, w2_hbm,
    out_ref,
    lat_v, c_v, gb,
    tmp, lat_t, raw, xc, xs1, xsc, acc1, part_out, part_in, mid, mid_in, x2, xs2, acc2,
    st1, st2, coef, rs_out, rs_in, w1, w2,
    isem, wsem, ls, lr, lr3, cs, cr, ss, kr, s1r, s2r, ns, hr, pr, mr, rsr, rf,
):
    row = lax.axis_index("rows")
    me = lax.axis_index("chan")
    M = T * W
    C2 = 2 * W
    H = M // 2
    HL = CL * T // 2
    OWN = Z - 1
    has_up = row > 0
    has_down = row < R - 1
    edge = jnp.logical_or(me == 0, me == Z - 1)
    inner = jnp.logical_not(edge)
    is_inner = ((me + 1) // 2) % 2

    def partner(k):
        other = me * 0
        bit = 1
        while bit < Z:
            mine = (me // bit) % 2
            other = other + bit * ((1 - mine) if k & bit else mine)
            bit *= 2
        return other

    barrier = pltpu.get_barrier_semaphore()
    for k in range(1, Z):
        pl.semaphore_signal(barrier, inc=1, device_id={"chan": partner(k)}, device_id_type=MESH)
    for k in range(1, R):
        pl.semaphore_signal(barrier, inc=1, device_id={"rows": lax.rem(row + k, R)}, device_id_type=MESH)

    lat_load = pltpu.make_async_copy(lat_hbm, lat_v, isem.at[0])
    loads = [
        lat_load,
        pltpu.make_async_copy(c1_hbm, c_v.at[0], isem.at[1]),
        pltpu.make_async_copy(c2_hbm, c_v.at[1], isem.at[1]),
    ] + [
        pltpu.make_async_copy(v, gb.at[pl.ds(i, 1)], isem.at[2])
        for i, v in enumerate((g1_hbm, b1_hbm, g2_hbm, b2_hbm))
    ]
    place = (0, 2, 1)
    w_copies = []
    for dt in range(3):
        for dh in range(3):
            w_copies.append(
                pltpu.make_async_copy(
                    w1_hbm.at[dt, dh],
                    w1.at[dt, :, :, pl.ds(place[dh] * CL, CL)],
                    wsem.at[0],
                )
            )
    w2_copy = pltpu.make_async_copy(w2_hbm, w2, wsem.at[1])
    lat_load.start()

    def wait_all(whole, sem):
        pltpu.make_async_copy(whole, whole, sem).wait()

    def to_chan(src, dst, send, recv, k):
        return pltpu.make_async_remote_copy(
            src_ref=src, dst_ref=dst, send_sem=send, recv_sem=recv,
            device_id={"chan": partner(k)}, device_id_type=MESH,
        )

    def to_row(src, dst, send, recv, k):
        return pltpu.make_async_remote_copy(
            src_ref=src, dst_ref=dst, send_sem=send, recv_sem=recv,
            device_id={"rows": lax.rem(row + k, R)}, device_id_type=MESH,
        )

    def along(src, buffer, send, recv, d, part, side):
        slot = OWN - side * d
        return pltpu.make_async_remote_copy(
            src_ref=src, dst_ref=buffer.at[(slot - side, *part)],
            send_sem=send, recv_sem=recv,
            device_id={"chan": me + side}, device_id_type=MESH,
        )

    def latent_hop(d, ch, side):
        slot = OWN - side * d
        rows = pl.ds(ch * HL, HL)
        src = lat_hbm.at[rows] if d == 0 else raw.at[slot, rows]
        way = (side + 1) // 2
        arrival = lr.at[way, d, ch] if d < 2 else lr3.at[way]
        return along(
            src, raw, ls.at[(side + 1) // 2, ch], arrival, d, (rows,), side
        )

    def cache_hop(d, side):
        slot = OWN - side * d
        return along(
            xc.at[slot], xc, cs.at[(side + 1) // 2], cr.at[(side + 1) // 2, d], d, (), side
        )

    def arrives(d, side):
        return me >= d if side > 0 else me + d <= Z - 1

    def goes(d, side):
        return jnp.logical_and(arrives(d, side), me < Z - 1 if side > 0 else me > 0)

    def also(here, some):
        return here if some is None else jnp.logical_and(here, some)

    def start_hop(hop, d, some=None):
        for side in (1, -1):

            @pl.when(also(goes(d, side), some))
            def _():
                if d > 0:
                    hop(d - 1, side).wait_send()
                hop(d, side).start()

    def wait_hop(hop, d, some=None):
        for side in (1, -1):

            @pl.when(also(arrives(d, side), some))
            def _():
                hop(d - 1, side).wait_recv()

    def wait_sent(hop, d, last=False):
        for side in (1, -1):
            here = goes(d, side)
            if last and d < Z - 2:
                here = jnp.logical_and(here, jnp.logical_not(goes(d + 1, side)))

            @pl.when(here)
            def _():
                hop(d, side).wait_send()

    def pass_on(hop, d, some=None):
        wait_hop(hop, d, some)
        if d < Z - 1:
            start_hop(hop, d, some)

    def latent_part(ch):
        return lambda d, side: latent_hop(d, ch, side)

    members = F32(R * M * (CHANNELS // GROUPS))
    gi = lax.broadcasted_iota(jnp.int32, (CL, CL), 0) // (CHANNELS // GROUPS)
    gj = lax.broadcasted_iota(jnp.int32, (CL, CL), 1) // (CHANNELS // GROUPS)
    same_group = (gi == gj).astype(BF16)

    def exact_dot(values, ones):
        terms = []
        for _ in range(3):
            terms.append(values.astype(BF16))
            values = values - terms[-1].astype(F32)
        count = terms[0].shape[0]
        out = jnp.dot(jnp.concatenate(terms, axis=0), ones, preferred_element_type=F32)
        return out[0:count] + out[count : 2 * count] + out[2 * count :]

    which = lax.broadcasted_iota(jnp.int32, (8, CL), 0)

    def local_stats(values):
        sums = jnp.sum(values, axis=0, keepdims=True)
        squares = jnp.sum(values * values, axis=0, keepdims=True)
        return jnp.where(which == 0, sums, jnp.where(which == 1, squares, 0.0))

    def share_stats(st, send, recv):
        for k in range(1, R):
            to_row(st.at[0, pl.ds(0, 2)], st.at[k, pl.ds(0, 2)], send, recv, k).start()

    def finish_stats(st, send, recv, gain):
        wait_all(st.at[pl.ds(1, R - 1), pl.ds(0, 2)], recv)
        wait_all(st.at[pl.ds(1, R - 1), pl.ds(0, 2)], send)
        total = st[0, 0:2, :]
        for k in range(1, R):
            total = total + st[k, 0:2, :]
        total = jnp.concatenate([total, jnp.zeros((6, CL), F32)], axis=0)
        total = exact_dot(total, same_group) / members
        mean = total[0:1, :]
        spread = jnp.maximum(total[1:2, :] - mean * mean, 0.0)
        return mean, lax.rsqrt(spread + epsilon) * gain

    def normed(values, coefs):
        mean, scale, bias = coefs
        u = (values - mean) * scale + bias
        return (u / (1.0 + jnp.exp(-u))).astype(BF16)

    def shifted(block):
        rows = block.shape[0]
        cell = lax.broadcasted_iota(jnp.int32, (rows, CL), 0) % W
        wide = block.astype(F32)
        left = jnp.where(cell == 0, 0.0, pltpu.roll(wide, 1, 0)).astype(BF16)
        right = jnp.where(cell == W - 1, 0.0, pltpu.roll(wide, rows - 1, 0)).astype(BF16)
        return left, block, right

    def put(dst, rows, column, block):
        for dx, value in enumerate(shifted(block)):
            dst[rows, column + dx * CL : column + (dx + 1) * CL] = value

    with jax.named_scope("barrier wait"):
        pl.semaphore_wait(barrier, R - 1 + Z - 1)

    start_hop(latent_part(0), 0)
    for copy in loads[1:] + w_copies:
        copy.start()

    halo_down = to_row(x2.at[1], x2.at[0], ns.at[0], hr.at[0], 1)
    halo_up = to_row(x2.at[1], x2.at[2], ns.at[1], hr.at[1], R - 1)

    with jax.named_scope("own latents"):
        lat_load.wait()
        tmp[...] = lat_v[...].astype(F32)
        for t in range(T):
            lat_t[t * W : (t + 1) * W, :] = tmp[pl.ds(t, CL, stride=T), :].T
        st1[0] = local_stats(lat_t[...])
        share_stats(st1, ss.at[0], s1r.at[0])

    with jax.named_scope("own caches"):
        wait_all(c_v, isem.at[1])
        for i, (buffer, slot) in enumerate(((xc, OWN), (x2, 1))):
            tmp[0 : 2 * CL, :] = c_v[i].astype(F32)
            for t in range(2):
                buffer[slot, t * W : (t + 1) * W, :] = (
                    tmp[pl.ds(t, CL, stride=2), :].T.astype(BF16)
                )
        acc1[...] = jnp.zeros_like(acc1)

    start_hop(latent_part(1), 0)

    @pl.when(has_down)
    def _():
        halo_down.start()

    @pl.when(has_up)
    def _():
        halo_up.start()

    def kernel_one(dt, z, low, high):
        base = pl.ds(pl.multiple_of(z * CL, CL), CL)
        return jnp.concatenate([w1[dt, dx, base, low:high] for dx in range(3)], axis=0)

    def latent_dots(z):
        for dt in (2, 1, 0):
            start = (2 - dt) * W
            acc1[start:, :] += jnp.dot(
                xs1[0 : M - start, :], kernel_one(dt, z, 0, 3 * CL), preferred_element_type=F32
            )

    def last_latent_dots(z, half, low, high):
        for dt in (2, 1, 0):
            first = half * H - (2 - dt) * W
            skip = max(0, -first)
            if skip < H:
                acc1[half * H + skip : (half + 1) * H, low:high] += jnp.dot(
                    xs1[first + skip : first + H, :], kernel_one(dt, z, low, high),
                    preferred_element_type=F32,
                )

    def cache_dots(z, low, high):
        for dt in range(2):
            acc1[0 : C2 - dt * W, low:high] += jnp.dot(
                xsc[dt * W : C2, :], kernel_one(dt, z, low, high), preferred_element_type=F32
            )

    def place_caches(slot):
        for t in range(2):
            rows = slice(t * W, (t + 1) * W)
            put(xsc, rows, 0, xc[slot, rows, :])

    def place_latents(slot, coefs):
        tmp[...] = raw[slot].astype(F32)
        for t in range(T):
            put(
                xs1, slice(t * W, (t + 1) * W), 0,
                normed(tmp[pl.ds(t, CL, stride=T), :].T, coefs),
            )

    def plane(k):
        if k == 1:
            return partner(1), 1
        a, b = partner(2), partner(3)
        if k == 2:
            return a + is_inner * (b - a), 2 + is_inner
        return b + is_inner * (a - b), 3 - is_inner

    def place_other(k):
        z, at = plane(k)
        place_latents(OWN + z - me, tuple(coef[at, i : i + 1, :] for i in range(3)))
        return z

    def other_latents(k):
        latent_dots(place_other(k))

    wait_all(w1, wsem.at[0])
    w2_copy.start()
    with jax.named_scope("own cache dots"):
        place_caches(OWN)
        cache_dots(me, 0, 3 * CL)
    start_hop(cache_hop, 0)

    with jax.named_scope("stats one"):
        wait_all(gb.at[pl.ds(0, 4)], isem.at[2])
        mean, scale = finish_stats(st1, ss.at[0], s1r.at[0], gb[0:1, :])
        bias = gb[1:2, :]
        coef[0] = jnp.where(which == 0, mean, jnp.where(which == 1, scale, bias))
        for k in range(1, Z):
            to_chan(coef.at[0], coef.at[k], ss.at[0], kr.at[0], k).start()

    with jax.named_scope("latents 1, part 0"):
        pass_on(latent_part(0), 1)

    with jax.named_scope("own latent dots"):
        for t in range(T):
            rows = slice(t * W, (t + 1) * W)
            put(xs1, rows, 0, normed(lat_t[rows, :], (mean, scale, bias)))
        latent_dots(me)
    with jax.named_scope("latents 1, part 1"):
        pass_on(latent_part(1), 1)
    with jax.named_scope("conv2 of caches"):
        w2_copy.wait()

        @pl.when(has_up)
        def _():
            halo_down.wait_recv()

        @pl.when(has_down)
        def _():
            halo_up.wait_recv()

        @pl.when(jnp.logical_not(has_up))
        def _():
            x2[0] = jnp.zeros((C2, CL), BF16)
            xs2[C2:, 0 : 3 * CL] = jnp.zeros((M, 3 * CL), BF16)

        @pl.when(jnp.logical_not(has_down))
        def _():
            x2[2] = jnp.zeros((C2, CL), BF16)
            xs2[C2:, 6 * CL :] = jnp.zeros((M, 3 * CL), BF16)

        for dh in range(3):
            put(xs2, slice(0, C2), dh * 3 * CL, x2[dh])
        both = jnp.dot(xs2[0:C2, :], w2[0], preferred_element_type=F32)
        one = jnp.dot(xs2[W:C2, :], w2[1], preferred_element_type=F32)
        for d in range(Z):
            cols = slice(d * CL, (d + 1) * CL)
            acc2[d, 0:W] = both[0:W, cols] + one[:, cols]
            acc2[d, W:C2] = both[W:C2, cols]
    with jax.named_scope("caches 1"):
        pass_on(cache_hop, 1)
    with jax.named_scope("latents 2, part 0"):
        pass_on(latent_part(0), 2)
    with jax.named_scope("latent dots 1"):
        wait_all(coef.at[pl.ds(1, Z - 1)], kr.at[0])
        other_latents(1)
    with jax.named_scope("latents 2, part 1"):
        pass_on(latent_part(1), 2)
    with jax.named_scope("latent dots 2"):
        other_latents(2)
    with jax.named_scope("caches 2"):
        pass_on(cache_hop, 2)
    with jax.named_scope("cache dots 1"):
        z, _ = plane(1)
        place_caches(OWN + z - me)
        cache_dots(z, 0, 3 * CL)
    with jax.named_scope("cache dots 2"):
        z, _ = plane(2)
        place_caches(OWN + z - me)
        cache_dots(z, 0, 3 * CL)

    with jax.named_scope("latents 3"):
        for side in (1, -1):

            @pl.when(arrives(Z - 1, side))
            def _():
                wait_all(raw.at[OWN - side * (Z - 1)], lr3.at[(side + 1) // 2])

    def rows_of(half):
        return slice(half * H, (half + 1) * H)

    def part_copies(half):
        rows = rows_of(half)
        return (
            to_row(part_out.at[0, rows], part_in.at[0, rows], ns.at[2 - 2 * half], pr.at[0, half], 1),
            to_row(part_out.at[1, rows], part_in.at[1, rows], ns.at[3 - 2 * half], pr.at[1, half], R - 1),
        )

    def mid_copies(half, t=0):
        rows = slice(t * W, (t + 1) * W) if half == 0 else rows_of(half)
        recv = hr if half else mr.at[t]
        return (
            to_row(mid.at[rows], mid_in.at[0, rows], ns.at[0], recv.at[0], 1),
            to_row(mid.at[rows], mid_in.at[1, rows], ns.at[1], recv.at[1], R - 1),
        )

    def start_rows(copies, before=()):
        for have, copy, old in zip((has_down, has_up), copies, before or (None, None)):

            @pl.when(have)
            def _():
                if old is not None:
                    old.wait_send()
                copy.start()

    def send_parts(half):
        rows = rows_of(half)
        part_out[0, rows] = acc1[rows, 0:CL].astype(BF16)
        part_out[1, rows] = acc1[rows, CL : 2 * CL].astype(BF16)
        start_rows(part_copies(half), (halo_down, halo_up) if half else ())

    def finish_mid(half):
        rows = rows_of(half)
        down, up = part_copies(half)

        @pl.when(has_up)
        def _():
            down.wait_recv()
            acc1[rows, 2 * CL :] += part_in[0, rows].astype(F32)

        @pl.when(has_down)
        def _():
            up.wait_recv()
            acc1[rows, 2 * CL :] += part_in[1, rows].astype(F32)

        mid[rows] = acc1[rows, 2 * CL :].astype(BF16)
        return local_stats(mid[rows].astype(F32))

    with jax.named_scope("parts of half 1"):
        z = place_other(3)
        last_latent_dots(z, 1, 0, 2 * CL)
        send_parts(1)
    with jax.named_scope("latent dots 3"):
        last_latent_dots(z, 0, 0, 2 * CL)
    with jax.named_scope("caches 3"):
        pass_on(cache_hop, 3)
    with jax.named_scope("cache dots 3"):
        z, _ = plane(3)
        place_caches(OWN + z - me)
        cache_dots(z, 0, 2 * CL)
        send_parts(0)
        last_latent_dots(z, 1, 2 * CL, 3 * CL)
        last_latent_dots(z, 0, 2 * CL, 3 * CL)
        cache_dots(z, 2 * CL, 3 * CL)
    with jax.named_scope("mid of half 1"):
        partial = finish_mid(1)
        start_rows(mid_copies(1), part_copies(1))

    with jax.named_scope("mid of half 0"):
        st2[0] = partial + finish_mid(0)
        wait_all(coef.at[pl.ds(1, Z - 1)], ss.at[0])
        share_stats(st2, ss.at[0], s2r.at[0])
        for t in range(2):
            start_rows(mid_copies(0, t))
        for hop in (latent_part(0), latent_part(1), cache_hop):
            for d in range(Z - 1):
                wait_sent(hop, d, last=True)
    with jax.named_scope("stats two"):
        coefs_two = (*finish_stats(st2, ss.at[0], s2r.at[0], gb[2:3, :]), gb[3:4, :])

    def place_mid(half, frames):
        down, up = mid_copies(half, frames[0] if half == 0 else 0)

        def place_row(dh, values):
            for t in frames:
                rows = slice(t * W, (t + 1) * W)
                there = slice(C2 + t * W, C2 + (t + 1) * W)
                put(xs2, there, dh * 3 * CL, normed(values[rows, :].astype(F32), coefs_two))

        place_row(1, mid)

        @pl.when(has_up)
        def _():
            down.wait_recv()
            place_row(0, mid_in.at[0])

        @pl.when(has_down)
        def _():
            up.wait_recv()
            place_row(2, mid_in.at[1])

    ZH = Z // 2
    mine = me // ZH

    def second_dots(frames, plane_at, planes=1):
        cols = pl.ds(pl.multiple_of(plane_at * CL, CL), planes * CL)
        start, end = frames[0] * W, (frames[-1] + 1) * W
        for dt in (2, 1, 0):
            back = (2 - dt) * W
            low = max(start, back)
            if low >= end:
                continue
            term = jnp.dot(
                xs2[C2 + low - back : C2 + end - back, :], w2[dt, :, cols],
                preferred_element_type=F32,
            )
            for j in range(planes):
                cut = term[:, j * CL : (j + 1) * CL]
                if start >= C2 and dt == 2:
                    acc2[plane_at + j, low:end] = cut
                else:
                    acc2[plane_at + j, low:end] += cut

    def frame(t):
        return slice(t * W, (t + 1) * W)

    def sum_copy(slot, half, k, to, rows=None):
        last = rows == frame(T - 1)
        rows = rows or rows_of(half)
        return to_chan(
            rs_out.at[k - 1, rows], rs_in.at[slot, rows],
            cs.at[half] if k == Z - 1 else ls.at[half, k - 1],
            rf.at[slot] if last and slot < Z - 1 else rsr.at[half, slot], to,
        )

    def send_sum(half, k, slot, to, rows=None):
        whole = rows or rows_of(half)
        rs_out[k - 1, whole] = acc2[partner(k), whole].astype(BF16)
        if half == 1 and k < Z - 1:
            for t in (T - 2, T - 1):
                sum_copy(slot, half, k, to, frame(t)).start()
        else:
            sum_copy(slot, half, k, to, rows).start()

    MERGE = 0

    def send_merged(half):
        for rows in (rows_of(0),) if half == 0 else (frame(T - 2), frame(T - 1)):
            sum_copy(MERGE, half, 3, 1, rows).wait_recv()
            rs_out[1, rows] = (acc2[partner(2), rows] + rs_in[MERGE, rows].astype(F32)).astype(BF16)
            sum_copy(2, half, 2, 2, rows).start()

    def send_far(half, rows=None):
        @pl.when(edge)
        def _():
            send_sum(half, 3, MERGE, 1, rows)

        @pl.when(inner)
        def _():
            send_sum(half, 3, 3, 3, rows)

    near = mine * ZH
    for t in range(T // 2):
        with jax.named_scope(f"place {t}"):
            place_mid(0, (t,))
        with jax.named_scope(f"conv2 far {t}"):
            second_dots((t,), partner(3))
            send_far(0, frame(t))

    with jax.named_scope("place half 1"):
        place_mid(1, (2, 3))
    with jax.named_scope("conv2 half 1 far"):
        for t in (T - 2, T - 1):
            second_dots((t,), partner(3))
            send_far(1, frame(t))

    with jax.named_scope("conv2 half 0 near"):
        second_dots((0, 1), near, ZH)
        send_sum(0, 1, 1, 1)

    with jax.named_scope("conv2 half 1 near"):
        second_dots((2, 3), near, ZH)
        send_sum(1, 1, 1, 1)
    with jax.named_scope("conv2 second far"):
        second_dots((0, 1), partner(2))
        second_dots((2, 3), partner(2))
        lat_t[...] = lat_t[...] + acc2[me]
    with jax.named_scope("last sums out"):

        @pl.when(edge)
        def _():
            for half in range(2):
                sum_copy(1, half, 1, 1).wait_send()
                send_sum(half, 2, 2, 2)

        @pl.when(inner)
        def _():
            for half in range(2):
                send_merged(half)

    ei = lax.broadcasted_iota(jnp.int32, (W, 2 * W), 0)
    ej = lax.broadcasted_iota(jnp.int32, (W, 2 * W), 1) // 2
    twice = (ei == ej).astype(BF16)

    def finish_frame(t):
        rows = frame(t)
        total = lat_t[rows, :] + rs_in[1, rows].astype(F32) + rs_in[2, rows].astype(F32)
        wide = exact_dot(total.T, twice)
        for side in range(2):
            for again in range(2):
                out_ref[pl.ds(t * 4 + side * 2 + again, CL, stride=4 * T), :] = wide[
                    :, side * W : (side + 1) * W
                ]

    for half in range(2):

        @pl.when(inner)
        def _():
            rows = rows_of(half)
            sum_copy(3, half, 3, 3).wait_recv()
            lat_t[rows, :] += rs_in[3, rows].astype(F32)

    with jax.named_scope("sums wait 0"):
        sum_copy(1, 0, 1, 1).wait_recv()
        sum_copy(2, 0, 2, 2).wait_recv()
    with jax.named_scope("upsample 0"):
        finish_frame(0)
        finish_frame(1)
    for t in (T - 2, T - 1):
        with jax.named_scope(f"sums wait {t}"):
            sum_copy(1, 1, 1, 1, frame(t)).wait_recv()
            sum_copy(2, 1, 2, 2, frame(t)).wait_recv()
        with jax.named_scope(f"upsample {t}"):
            finish_frame(t)

    with jax.named_scope("sends wait"):
        for half in range(2):
            sum_copy(1, half, 3, 1).wait_send()
            sum_copy(2, half, 2, 2).wait_send()

            @pl.when(inner)
            def _():
                sum_copy(1, half, 1, 1).wait_send()

        for have, way in ((has_down, 0), (has_up, 1)):

            @pl.when(have)
            def _():
                part_copies(0)[way].wait_send()
                wait_all(mid, ns.at[way])


def body(
    latents, cache_one, cache_two, gain_one, bias_one, weight_one, gain_two, bias_two, weight_two
):
    CL, T, rows_here, W = latents.shape
    R, Z = lax.axis_size("rows"), lax.axis_size("chan")
    if CL != 128 or W != 128 or rows_here != 1 or T != 4 or R < 2 or Z != 4:
        return plain_body(
            latents, cache_one, cache_two, gain_one, bias_one, weight_one, gain_two, bias_two,
            weight_two,
        )
    C = CL * Z
    M = T * W
    hbm = pl.BlockSpec(memory_space=pltpu.HBM)
    dma = pltpu.SemaphoreType.DMA
    out = pl.pallas_call(
        functools.partial(block_kernel, R, Z, CL, T, W),
        out_shape=jax.ShapeDtypeStruct((CL * T * 4, W), F32),
        in_specs=[hbm] * 9,
        out_specs=pl.BlockSpec(memory_space=pltpu.VMEM),
        scratch_shapes=[
            pltpu.VMEM((CL * T, W), BF16),
            pltpu.VMEM((2, CL * 2, W), BF16),
            pltpu.VMEM((8, CL), F32),
            pltpu.VMEM((CL * T, W), F32),
            pltpu.VMEM((M, CL), F32),
            pltpu.VMEM((2 * Z - 1, CL * T, W), BF16),
            pltpu.VMEM((2 * Z - 1, 2 * W, CL), BF16),
            pltpu.VMEM((M, 3 * CL), BF16),
            pltpu.VMEM((2 * W, 3 * CL), BF16),
            pltpu.VMEM((M, 3 * CL), F32),
            pltpu.VMEM((2, M, CL), BF16),
            pltpu.VMEM((2, M, CL), BF16),
            pltpu.VMEM((M, CL), BF16),
            pltpu.VMEM((2, M, CL), BF16),
            pltpu.VMEM((3, 2 * W, CL), BF16),
            pltpu.VMEM((M + 2 * W, 9 * CL), BF16),
            pltpu.VMEM((Z, M, CL), F32),
            pltpu.VMEM((R, 8, CL), F32),
            pltpu.VMEM((R, 8, CL), F32),
            pltpu.VMEM((Z, 8, CL), F32),
            pltpu.VMEM((Z - 1, M, CL), BF16),
            pltpu.VMEM((Z, M, CL), BF16),
            pltpu.VMEM((3, 3, C, 3 * CL), BF16),
            pltpu.VMEM((3, 9 * CL, C), BF16),
            dma((3,)), dma((2,)),
            dma((2, 2)), dma((2, 2, 2)), dma((2,)),
            dma((2,)), dma((2, Z - 1)),
            dma((1,)), dma((1,)), dma((1,)), dma((1,)),
            dma((4,)), dma((2,)), dma((2, 2)), dma((2, 2)),
            dma((2, Z)), dma((3,)),
        ],
        compiler_params=pltpu.CompilerParams(
            collective_id=0, has_side_effects=True, vmem_limit_bytes=40 * 1024 * 1024
        ),
    )(*(pltpu.with_memory_space_constraint(v, pltpu.HBM) for v in (
        latents.reshape(CL * T, W),
        cache_one.reshape(CL * 2, W),
        cache_two.reshape(CL * 2, W),
        gain_one.reshape(1, CL),
        bias_one.reshape(1, CL),
        gain_two.reshape(1, CL),
        bias_two.reshape(1, CL),
        weight_one,
        weight_two.reshape(3, 9 * CL, C),
    )))
    return out.reshape(CL, T, 2, 2, W).transpose(0, 1, 3, 2, 4).reshape(CL, T, 2, 2 * W)


def solution(mesh):
    return jax.shard_map(
        body,
        mesh=mesh,
        in_specs=(
            P("chan", None, "rows", None),
            P("chan", None, "rows", None),
            P("chan", None, "rows", None),
            P("chan"),
            P("chan"),
            P(None, None, None, None, "chan"),
            P("chan"),
            P("chan"),
            P(None, None, None, "chan", None),
        ),
        out_specs=P("chan", None, "rows", None),
        check_vma=False,
    )
```

```python
import functools

import jax
import jax.numpy as jnp
from jax import lax
from jax.experimental import pallas as pl
from jax.experimental.pallas import tpu as pltpu
from jax.sharding import PartitionSpec as P

CHANNELS = 512
GROUPS = 32
MESH = pl.DeviceIdType.MESH
F32 = jnp.float32
BF16 = jnp.bfloat16


epsilon = 1e-06


def padded(block, sides, width):
    for axis, dim in sides:
        count = lax.axis_size(axis)
        forward = [(i, i + 1) for i in range(count - 1)]
        backward = [(target, source) for source, target in forward]
        low = lax.ppermute(
            lax.slice_in_dim(block, block.shape[dim] - width, None, axis=dim), axis, forward
        )
        high = lax.ppermute(lax.slice_in_dim(block, 0, width, axis=dim), axis, backward)
        block = jnp.concatenate([low, block, high], axis=dim)
    return block


def group_silu(values, gain, bias):
    group_size = CHANNELS // GROUPS
    grouped = values.reshape(values.shape[0] // group_size, -1)
    sums, squares = lax.psum((jnp.sum(grouped, axis=1), jnp.sum(grouped * grouped, axis=1)), "rows")
    members = grouped.shape[1] * lax.axis_size("rows")
    average = sums / members
    spread = squares / members - average * average
    normed = ((grouped - average[:, None]) * lax.rsqrt(spread + epsilon)[:, None]).reshape(
        values.shape
    )
    scaled = normed * gain[:, None, None, None] + bias[:, None, None, None]
    return jax.nn.silu(scaled).astype(jnp.bfloat16)


def pad_rows(frames):
    return padded(frames, (("rows", 2),), 1)


def conv_block(frames, kernel):
    result = lax.conv_general_dilated(
        frames[None],
        kernel,
        (1, 1, 1),
        ((0, 0), (0, 0), (1, 1)),
        dimension_numbers=("NCDHW", "DHWIO", "NCDHW"),
        preferred_element_type=jnp.float32,
    )
    return result[0]


def gathered_conv(frames, kernel):
    channels = lax.all_gather(frames, "chan", axis=0, tiled=True)
    return conv_block(channels, kernel)


def plain_body(
    latents, cache_one, cache_two, gain_one, bias_one, weight_one, gain_two, bias_two, weight_two
):
    floats = latents.astype(jnp.float32)
    first = group_silu(floats, gain_one, bias_one)
    frames_one = pad_rows(jnp.concatenate([cache_one, first], axis=1))
    middle = gathered_conv(frames_one, weight_one).astype(jnp.bfloat16)
    second = group_silu(middle.astype(jnp.float32), gain_two, bias_two)
    frames_two = pad_rows(jnp.concatenate([cache_two, second], axis=1))
    columns = lax.all_to_all(weight_two, "chan", split_axis=4, concat_axis=3, tiled=True)
    result = floats + gathered_conv(frames_two, columns)
    return jnp.repeat(jnp.repeat(result, 2, axis=2), 2, axis=3)


def block_kernel(
    R, Z, CL, T, W,
    lat_hbm, c1_hbm, c2_hbm, g1_hbm, b1_hbm, g2_hbm, b2_hbm, w1_hbm, w2_hbm,
    out_ref,
    lat_v, c_v, gb,
    tmp, lat_t, raw, xc, xs1, xsc, acc1, part_out, part_in, mid, mid_in, x2, xs2, acc2,
    st1, st2, coef, rs_out, rs_in, w1, w2, ahead,
    isem, wsem, ls, lr, lr3, cs, cr, ss, kr, s1r, s2r, ns, hr, pr, mr, rsr, rf,
):
    row = lax.axis_index("rows")
    me = lax.axis_index("chan")
    M = T * W
    C2 = 2 * W
    H = M // 2
    HL = CL * T // 2
    OWN = Z - 1
    has_up = row > 0
    has_down = row < R - 1
    edge = jnp.logical_or(me == 0, me == Z - 1)
    inner = jnp.logical_not(edge)
    is_inner = ((me + 1) // 2) % 2

    def partner(k):
        other = me * 0
        bit = 1
        while bit < Z:
            mine = (me // bit) % 2
            other = other + bit * ((1 - mine) if k & bit else mine)
            bit *= 2
        return other

    barrier = pltpu.get_barrier_semaphore()
    for k in range(1, Z):
        pl.semaphore_signal(barrier, inc=1, device_id={"chan": partner(k)}, device_id_type=MESH)
    for k in range(1, R):
        pl.semaphore_signal(barrier, inc=1, device_id={"rows": lax.rem(row + k, R)}, device_id_type=MESH)

    lat_load = pltpu.make_async_copy(lat_hbm, lat_v, isem.at[0])
    loads = [
        lat_load,
        pltpu.make_async_copy(c1_hbm, c_v.at[0], isem.at[1]),
        pltpu.make_async_copy(c2_hbm, c_v.at[1], isem.at[1]),
    ] + [
        pltpu.make_async_copy(v, gb.at[pl.ds(i, 1)], isem.at[2])
        for i, v in enumerate((g1_hbm, b1_hbm, g2_hbm, b2_hbm))
    ]
    place = (0, 2, 1)
    w_copies = []
    for dt in range(3):
        for dh in range(3):
            w_copies.append(
                pltpu.make_async_copy(
                    w1_hbm.at[dt, dh],
                    w1.at[dt, :, :, pl.ds(place[dh] * CL, CL)],
                    wsem.at[0],
                )
            )
    w2_copy = pltpu.make_async_copy(w2_hbm, w2, wsem.at[1])
    lat_load.start()

    def wait_all(whole, sem):
        pltpu.make_async_copy(whole, whole, sem).wait()

    def to_chan(src, dst, send, recv, k):
        return pltpu.make_async_remote_copy(
            src_ref=src, dst_ref=dst, send_sem=send, recv_sem=recv,
            device_id={"chan": partner(k)}, device_id_type=MESH,
        )

    def to_row(src, dst, send, recv, k):
        return pltpu.make_async_remote_copy(
            src_ref=src, dst_ref=dst, send_sem=send, recv_sem=recv,
            device_id={"rows": lax.rem(row + k, R)}, device_id_type=MESH,
        )

    def along(src, buffer, send, recv, d, part, side):
        slot = OWN - side * d
        return pltpu.make_async_remote_copy(
            src_ref=src, dst_ref=buffer.at[(slot - side, *part)],
            send_sem=send, recv_sem=recv,
            device_id={"chan": me + side}, device_id_type=MESH,
        )

    def latent_hop(d, ch, side):
        slot = OWN - side * d
        rows = pl.ds(ch * HL, HL)
        src = lat_hbm.at[rows] if d == 0 else raw.at[slot, rows]
        way = (side + 1) // 2
        arrival = lr.at[way, d, ch] if d < 2 else lr3.at[way]
        return along(
            src, raw, ls.at[(side + 1) // 2, ch], arrival, d, (rows,), side
        )

    def cache_hop(d, side):
        slot = OWN - side * d
        return along(
            xc.at[slot], xc, cs.at[(side + 1) // 2], cr.at[(side + 1) // 2, d], d, (), side
        )

    def arrives(d, side):
        return me >= d if side > 0 else me + d <= Z - 1

    def goes(d, side):
        return jnp.logical_and(arrives(d, side), me < Z - 1 if side > 0 else me > 0)

    def also(here, some):
        return here if some is None else jnp.logical_and(here, some)

    def start_hop(hop, d, some=None):
        for side in (1, -1):

            @pl.when(also(goes(d, side), some))
            def _():
                if d > 0:
                    hop(d - 1, side).wait_send()
                hop(d, side).start()

    def wait_hop(hop, d, some=None):
        for side in (1, -1):

            @pl.when(also(arrives(d, side), some))
            def _():
                hop(d - 1, side).wait_recv()

    def wait_sent(hop, d, last=False):
        for side in (1, -1):
            here = goes(d, side)
            if last and d < Z - 2:
                here = jnp.logical_and(here, jnp.logical_not(goes(d + 1, side)))

            @pl.when(here)
            def _():
                hop(d, side).wait_send()

    def pass_on(hop, d, some=None):
        wait_hop(hop, d, some)
        if d < Z - 1:
            start_hop(hop, d, some)

    def latent_part(ch):
        return lambda d, side: latent_hop(d, ch, side)

    members = F32(R * M * (CHANNELS // GROUPS))
    gi = lax.broadcasted_iota(jnp.int32, (CL, CL), 0) // (CHANNELS // GROUPS)
    gj = lax.broadcasted_iota(jnp.int32, (CL, CL), 1) // (CHANNELS // GROUPS)
    same_group = (gi == gj).astype(BF16)

    def exact_dot(values, ones):
        terms = []
        for _ in range(3):
            terms.append(values.astype(BF16))
            values = values - terms[-1].astype(F32)
        count = terms[0].shape[0]
        out = jnp.dot(jnp.concatenate(terms, axis=0), ones, preferred_element_type=F32)
        return out[0:count] + out[count : 2 * count] + out[2 * count :]

    which = lax.broadcasted_iota(jnp.int32, (8, CL), 0)

    def local_stats(values):
        sums = jnp.sum(values, axis=0, keepdims=True)
        squares = jnp.sum(values * values, axis=0, keepdims=True)
        return jnp.where(which == 0, sums, jnp.where(which == 1, squares, 0.0))

    def share_stats(st, send, recv):
        for k in range(1, R):
            to_row(st.at[0, pl.ds(0, 2)], st.at[k, pl.ds(0, 2)], send, recv, k).start()

    def finish_stats(st, send, recv, gain):
        wait_all(st.at[pl.ds(1, R - 1), pl.ds(0, 2)], recv)
        wait_all(st.at[pl.ds(1, R - 1), pl.ds(0, 2)], send)
        total = st[0, 0:2, :]
        for k in range(1, R):
            total = total + st[k, 0:2, :]
        total = jnp.concatenate([total, jnp.zeros((6, CL), F32)], axis=0)
        total = exact_dot(total, same_group) / members
        mean = total[0:1, :]
        spread = jnp.maximum(total[1:2, :] - mean * mean, 0.0)
        return mean, lax.rsqrt(spread + epsilon) * gain

    def normed(values, coefs):
        mean, scale, bias = coefs
        u = (values - mean) * scale + bias
        return (u / (1.0 + jnp.exp(-u))).astype(BF16)

    def shifted(block):
        rows = block.shape[0]
        cell = lax.broadcasted_iota(jnp.int32, (rows, CL), 0) % W
        wide = block.astype(F32)
        left = jnp.where(cell == 0, 0.0, pltpu.roll(wide, 1, 0)).astype(BF16)
        right = jnp.where(cell == W - 1, 0.0, pltpu.roll(wide, rows - 1, 0)).astype(BF16)
        return left, block, right

    def put(dst, rows, column, block):
        for dx, value in enumerate(shifted(block)):
            dst[rows, column + dx * CL : column + (dx + 1) * CL] = value

    with jax.named_scope("barrier wait"):
        pl.semaphore_wait(barrier, R - 1 + Z - 1)

    start_hop(latent_part(0), 0)
    for copy in loads[1:] + w_copies:
        copy.start()

    halo_down = to_row(x2.at[1], x2.at[0], ns.at[0], hr.at[0], 1)
    halo_up = to_row(x2.at[1], x2.at[2], ns.at[1], hr.at[1], R - 1)

    with jax.named_scope("own latents"):
        lat_load.wait()
        tmp[...] = lat_v[...].astype(F32)
        for t in range(T):
            lat_t[t * W : (t + 1) * W, :] = tmp[pl.ds(t, CL, stride=T), :].T
        st1[0] = local_stats(lat_t[...])
        share_stats(st1, ss.at[0], s1r.at[0])

    with jax.named_scope("own caches"):
        wait_all(c_v, isem.at[1])
        for i, (buffer, slot) in enumerate(((xc, OWN), (x2, 1))):
            tmp[0 : 2 * CL, :] = c_v[i].astype(F32)
            for t in range(2):
                buffer[slot, t * W : (t + 1) * W, :] = (
                    tmp[pl.ds(t, CL, stride=2), :].T.astype(BF16)
                )
        acc1[...] = jnp.zeros_like(acc1)

    start_hop(latent_part(1), 0)

    @pl.when(has_down)
    def _():
        halo_down.start()

    @pl.when(has_up)
    def _():
        halo_up.start()

    def kernel_one(dt, z, low, high):
        base = pl.ds(pl.multiple_of(z * CL, CL), CL)
        return jnp.concatenate([w1[dt, dx, base, low:high] for dx in range(3)], axis=0)

    def latent_dots(z):
        for dt in (2, 1, 0):
            start = (2 - dt) * W
            acc1[start:, :] += jnp.dot(
                xs1[0 : M - start, :], kernel_one(dt, z, 0, 3 * CL), preferred_element_type=F32
            )

    def last_latent_dots(z, half, low, high):
        for dt in (2, 1, 0):
            first = half * H - (2 - dt) * W
            skip = max(0, -first)
            if skip < H:
                acc1[half * H + skip : (half + 1) * H, low:high] += jnp.dot(
                    xs1[first + skip : first + H, :], kernel_one(dt, z, low, high),
                    preferred_element_type=F32,
                )

    def cache_dots(z, low, high):
        for dt in range(2):
            acc1[0 : C2 - dt * W, low:high] += jnp.dot(
                xsc[dt * W : C2, :], kernel_one(dt, z, low, high), preferred_element_type=F32
            )

    def place_caches(slot):
        for t in range(2):
            rows = slice(t * W, (t + 1) * W)
            put(xsc, rows, 0, xc[slot, rows, :])

    def place_latents(slot, coefs):
        tmp[...] = raw[slot].astype(F32)
        for t in range(T):
            put(
                xs1, slice(t * W, (t + 1) * W), 0,
                normed(tmp[pl.ds(t, CL, stride=T), :].T, coefs),
            )

    def plane(k):
        if k == 1:
            return partner(1), 1
        a, b = partner(2), partner(3)
        if k == 2:
            return a + is_inner * (b - a), 2 + is_inner
        return b + is_inner * (a - b), 3 - is_inner

    def place_other(k):
        z, at = plane(k)
        place_latents(OWN + z - me, tuple(coef[at, i : i + 1, :] for i in range(3)))
        return z

    def other_latents(k):
        latent_dots(place_other(k))

    wait_all(w1, wsem.at[0])
    w2_copy.start()
    with jax.named_scope("own cache dots"):
        place_caches(OWN)
        cache_dots(me, 0, 3 * CL)
    start_hop(cache_hop, 0)

    with jax.named_scope("stats one"):
        wait_all(gb.at[pl.ds(0, 4)], isem.at[2])
        mean, scale = finish_stats(st1, ss.at[0], s1r.at[0], gb[0:1, :])
        bias = gb[1:2, :]
        coef[0] = jnp.where(which == 0, mean, jnp.where(which == 1, scale, bias))
        for k in range(1, Z):
            to_chan(coef.at[0], coef.at[k], ss.at[0], kr.at[0], k).start()

    with jax.named_scope("latents 1, part 0"):
        pass_on(latent_part(0), 1)

    with jax.named_scope("own latent dots"):
        for t in range(T):
            rows = slice(t * W, (t + 1) * W)
            put(xs1, rows, 0, normed(lat_t[rows, :], (mean, scale, bias)))
        latent_dots(me)
    with jax.named_scope("latents 1, part 1"):
        pass_on(latent_part(1), 1)
    with jax.named_scope("conv2 of caches"):
        w2_copy.wait()

        @pl.when(has_up)
        def _():
            halo_down.wait_recv()

        @pl.when(has_down)
        def _():
            halo_up.wait_recv()

        @pl.when(jnp.logical_not(has_up))
        def _():
            x2[0] = jnp.zeros((C2, CL), BF16)
            xs2[C2:, 0 : 3 * CL] = jnp.zeros((M, 3 * CL), BF16)

        @pl.when(jnp.logical_not(has_down))
        def _():
            x2[2] = jnp.zeros((C2, CL), BF16)
            xs2[C2:, 6 * CL :] = jnp.zeros((M, 3 * CL), BF16)

        for dh in range(3):
            put(xs2, slice(0, C2), dh * 3 * CL, x2[dh])
        both = jnp.dot(xs2[0:C2, :], w2[0], preferred_element_type=F32)
        one = jnp.dot(xs2[W:C2, :], w2[1], preferred_element_type=F32)
        for d in range(Z):
            cols = slice(d * CL, (d + 1) * CL)
            acc2[d, 0:W] = both[0:W, cols] + one[:, cols]
            acc2[d, W:C2] = both[W:C2, cols]
    with jax.named_scope("caches 1"):
        pass_on(cache_hop, 1)
    with jax.named_scope("latents 2, part 0"):
        pass_on(latent_part(0), 2)
    with jax.named_scope("latent dots 1"):
        wait_all(coef.at[pl.ds(1, Z - 1)], kr.at[0])
        other_latents(1)
    with jax.named_scope("latents 2, part 1"):
        pass_on(latent_part(1), 2)
    with jax.named_scope("latent dots 2"):
        other_latents(2)
    with jax.named_scope("caches 2"):
        pass_on(cache_hop, 2)
    with jax.named_scope("cache dots 1"):
        z, _ = plane(1)
        place_caches(OWN + z - me)
        cache_dots(z, 0, 3 * CL)
    with jax.named_scope("cache dots 2"):
        z, _ = plane(2)
        place_caches(OWN + z - me)
        cache_dots(z, 0, 3 * CL)

    with jax.named_scope("latents 3"):
        for side in (1, -1):

            @pl.when(arrives(Z - 1, side))
            def _():
                wait_all(raw.at[OWN - side * (Z - 1)], lr3.at[(side + 1) // 2])

    def rows_of(half):
        return slice(half * H, (half + 1) * H)

    def part_copies(half):
        rows = rows_of(half)
        return (
            to_row(part_out.at[0, rows], part_in.at[0, rows], ns.at[2 - 2 * half], pr.at[0, half], 1),
            to_row(part_out.at[1, rows], part_in.at[1, rows], ns.at[3 - 2 * half], pr.at[1, half], R - 1),
        )

    def mid_copies(half, t=0):
        rows = slice(t * W, (t + 1) * W) if half == 0 else rows_of(half)
        recv = hr if half else mr.at[t]
        return (
            to_row(mid.at[rows], mid_in.at[0, rows], ns.at[0], recv.at[0], 1),
            to_row(mid.at[rows], mid_in.at[1, rows], ns.at[1], recv.at[1], R - 1),
        )

    def start_rows(copies, before=()):
        for have, copy, old in zip((has_down, has_up), copies, before or (None, None)):

            @pl.when(have)
            def _():
                if old is not None:
                    old.wait_send()
                copy.start()

    def send_parts(half):
        rows = rows_of(half)
        part_out[0, rows] = acc1[rows, 0:CL].astype(BF16)
        part_out[1, rows] = acc1[rows, CL : 2 * CL].astype(BF16)
        start_rows(part_copies(half), (halo_down, halo_up) if half else ())

    def finish_mid(half):
        rows = rows_of(half)
        down, up = part_copies(half)

        @pl.when(has_up)
        def _():
            down.wait_recv()
            acc1[rows, 2 * CL :] += part_in[0, rows].astype(F32)

        @pl.when(has_down)
        def _():
            up.wait_recv()
            acc1[rows, 2 * CL :] += part_in[1, rows].astype(F32)

        mid[rows] = acc1[rows, 2 * CL :].astype(BF16)
        return local_stats(mid[rows].astype(F32))

    with jax.named_scope("parts of half 1"):
        z = place_other(3)
        last_latent_dots(z, 1, 0, 2 * CL)
        send_parts(1)
    with jax.named_scope("latent dots 3"):
        last_latent_dots(z, 0, 0, 2 * CL)
    with jax.named_scope("caches 3"):
        pass_on(cache_hop, 3)
    with jax.named_scope("cache dots 3"):
        z, _ = plane(3)
        place_caches(OWN + z - me)
        cache_dots(z, 0, 2 * CL)
        send_parts(0)
        last_latent_dots(z, 1, 2 * CL, 3 * CL)
        last_latent_dots(z, 0, 2 * CL, 3 * CL)
        cache_dots(z, 2 * CL, 3 * CL)
    with jax.named_scope("mid of half 1"):
        partial = finish_mid(1)
        start_rows(mid_copies(1), part_copies(1))

    with jax.named_scope("mid of half 0"):
        st2[0] = partial + finish_mid(0)
        wait_all(coef.at[pl.ds(1, Z - 1)], ss.at[0])
        share_stats(st2, ss.at[0], s2r.at[0])
        for t in range(2):
            start_rows(mid_copies(0, t))
        for hop in (latent_part(0), latent_part(1), cache_hop):
            for d in range(Z - 1):
                wait_sent(hop, d, last=True)
    with jax.named_scope("stats two"):
        coefs_two = (*finish_stats(st2, ss.at[0], s2r.at[0], gb[2:3, :]), gb[3:4, :])

    def place_mid(half, frames):
        down, up = mid_copies(half, frames[0] if half == 0 else 0)

        def place_row(dh, values):
            for t in frames:
                rows = slice(t * W, (t + 1) * W)
                there = slice(C2 + t * W, C2 + (t + 1) * W)
                put(xs2, there, dh * 3 * CL, normed(values[rows, :].astype(F32), coefs_two))

        place_row(1, mid)

        @pl.when(has_up)
        def _():
            down.wait_recv()
            place_row(0, mid_in.at[0])

        @pl.when(has_down)
        def _():
            up.wait_recv()
            place_row(2, mid_in.at[1])

    ZH = Z // 2
    mine = me // ZH

    def second_dots(frames, plane_at, planes=1):
        cols = pl.ds(pl.multiple_of(plane_at * CL, CL), planes * CL)
        start, end = frames[0] * W, (frames[-1] + 1) * W
        for dt in (2, 1, 0):
            back = (2 - dt) * W
            low = max(start, back)
            if low >= end:
                continue
            term = jnp.dot(
                xs2[C2 + low - back : C2 + end - back, :], w2[dt, :, cols],
                preferred_element_type=F32,
            )
            for j in range(planes):
                cut = term[:, j * CL : (j + 1) * CL]
                if start >= C2 and dt == 2:
                    acc2[plane_at + j, low:end] = cut
                else:
                    acc2[plane_at + j, low:end] += cut

    MERGE = 0

    def frame(t):
        return slice(t * W, (t + 1) * W)

    def sum_copy(slot, half, k, to, rows=None):
        arrival = rsr.at[half, slot]
        if rows == frame(T - 1) and slot < Z - 1:
            arrival = rf.at[slot]
        if rows == frame(1) and slot == MERGE:
            arrival = rf.at[Z - 1]
        rows = rows or rows_of(half)
        return to_chan(
            rs_out.at[k - 1, rows], rs_in.at[slot, rows],
            cs.at[half] if k == Z - 1 else ls.at[half, k - 1],
            arrival, to,
        )

    def send_sum(half, k, slot, to, rows=None):
        whole = rows or rows_of(half)
        rs_out[k - 1, whole] = acc2[partner(k), whole].astype(BF16)
        if half == 1 and k < Z - 1:
            for t in (T - 2, T - 1):
                sum_copy(slot, half, k, to, frame(t)).start()
        else:
            sum_copy(slot, half, k, to, rows).start()

    def send_merged(half):
        for rows in (frame(2 * half), frame(2 * half + 1)):
            sum_copy(MERGE, half, 3, 1, rows).wait_recv()
            rs_out[1, rows] = (acc2[partner(2), rows] + rs_in[MERGE, rows].astype(F32)).astype(BF16)
            sum_copy(2, half, 2, 2, rows).start()

    def send_far(half, rows=None):
        @pl.when(edge)
        def _():
            send_sum(half, 3, MERGE, 1, rows)

        @pl.when(inner)
        def _():
            send_sum(half, 3, 3, 3, rows)

    near = mine * ZH
    for t in range(T // 2):
        with jax.named_scope(f"place {t}"):
            place_mid(0, (t,))
        with jax.named_scope(f"conv2 far {t}"):
            second_dots((t,), partner(3))
            send_far(0, frame(t))

    with jax.named_scope("place half 1"):
        place_mid(1, (2, 3))
    with jax.named_scope("conv2 half 1 far"):
        for t in (T - 2, T - 1):
            second_dots((t,), partner(3))
            send_far(1, frame(t))

    with jax.named_scope("conv2 half 0 near"):
        second_dots((0, 1), near, ZH)
        send_sum(0, 1, 1, 1)

    with jax.named_scope("conv2 half 1 near"):
        second_dots((2, 3), near, ZH)
        send_sum(1, 1, 1, 1)
    with jax.named_scope("conv2 second far"):
        second_dots((0, 1), partner(2))
        second_dots((2, 3), partner(2))
        lat_t[...] = lat_t[...] + acc2[me]
    with jax.named_scope("last sums out"):

        @pl.when(edge)
        def _():
            for half in range(2):
                sum_copy(1, half, 1, 1).wait_send()
                send_sum(half, 2, 2, 2)

        @pl.when(inner)
        def _():
            for half in range(2):
                send_merged(half)

    ei = lax.broadcasted_iota(jnp.int32, (W, 2 * W), 0)
    ej = lax.broadcasted_iota(jnp.int32, (W, 2 * W), 1) // 2
    twice = (ei == ej).astype(BF16)

    def prepare_frame(t):
        rows = frame(t)
        ahead[t % 2] = exact_dot((lat_t[rows, :] + rs_in[1, rows].astype(F32)).T, twice)

    def finish_frame(t):
        wide = ahead[t % 2] + jnp.dot(
            rs_in[2, frame(t)].T, twice, preferred_element_type=F32
        )
        for side in range(2):
            for again in range(2):
                out_ref[pl.ds(t * 4 + side * 2 + again, CL, stride=4 * T), :] = wide[
                    :, side * W : (side + 1) * W
                ]

    for half in range(2):

        @pl.when(inner)
        def _():
            rows = rows_of(half)
            sum_copy(3, half, 3, 3).wait_recv()
            lat_t[rows, :] += rs_in[3, rows].astype(F32)

    with jax.named_scope("sums wait 0"):
        sum_copy(1, 0, 1, 1).wait_recv()
        prepare_frame(0)
        prepare_frame(1)
        sum_copy(2, 0, 2, 2).wait_recv()
    with jax.named_scope("upsample 0"):
        finish_frame(0)
        finish_frame(1)
    with jax.named_scope("near sums 1"):
        for t in (T - 2, T - 1):
            sum_copy(1, 1, 1, 1, frame(t)).wait_recv()
            prepare_frame(t)
    for t in (T - 2, T - 1):
        with jax.named_scope(f"sums wait {t}"):
            sum_copy(2, 1, 2, 2, frame(t)).wait_recv()
        with jax.named_scope(f"upsample {t}"):
            finish_frame(t)

    with jax.named_scope("sends wait"):
        for half in range(2):
            sum_copy(1, half, 3, 1).wait_send()
            sum_copy(2, half, 2, 2).wait_send()

            @pl.when(inner)
            def _():
                sum_copy(1, half, 1, 1).wait_send()

        for have, way in ((has_down, 0), (has_up, 1)):

            @pl.when(have)
            def _():
                part_copies(0)[way].wait_send()
                wait_all(mid, ns.at[way])


def body(
    latents, cache_one, cache_two, gain_one, bias_one, weight_one, gain_two, bias_two, weight_two
):
    CL, T, rows_here, W = latents.shape
    R, Z = lax.axis_size("rows"), lax.axis_size("chan")
    if CL != 128 or W != 128 or rows_here != 1 or T != 4 or R < 2 or Z != 4:
        return plain_body(
            latents, cache_one, cache_two, gain_one, bias_one, weight_one, gain_two, bias_two,
            weight_two,
        )
    C = CL * Z
    M = T * W
    hbm = pl.BlockSpec(memory_space=pltpu.HBM)
    dma = pltpu.SemaphoreType.DMA
    out = pl.pallas_call(
        functools.partial(block_kernel, R, Z, CL, T, W),
        out_shape=jax.ShapeDtypeStruct((CL * T * 4, W), F32),
        in_specs=[hbm] * 9,
        out_specs=pl.BlockSpec(memory_space=pltpu.VMEM),
        scratch_shapes=[
            pltpu.VMEM((CL * T, W), BF16),
            pltpu.VMEM((2, CL * 2, W), BF16),
            pltpu.VMEM((8, CL), F32),
            pltpu.VMEM((CL * T, W), F32),
            pltpu.VMEM((M, CL), F32),
            pltpu.VMEM((2 * Z - 1, CL * T, W), BF16),
            pltpu.VMEM((2 * Z - 1, 2 * W, CL), BF16),
            pltpu.VMEM((M, 3 * CL), BF16),
            pltpu.VMEM((2 * W, 3 * CL), BF16),
            pltpu.VMEM((M, 3 * CL), F32),
            pltpu.VMEM((2, M, CL), BF16),
            pltpu.VMEM((2, M, CL), BF16),
            pltpu.VMEM((M, CL), BF16),
            pltpu.VMEM((2, M, CL), BF16),
            pltpu.VMEM((3, 2 * W, CL), BF16),
            pltpu.VMEM((M + 2 * W, 9 * CL), BF16),
            pltpu.VMEM((Z, M, CL), F32),
            pltpu.VMEM((R, 8, CL), F32),
            pltpu.VMEM((R, 8, CL), F32),
            pltpu.VMEM((Z, 8, CL), F32),
            pltpu.VMEM((Z - 1, M, CL), BF16),
            pltpu.VMEM((Z, M, CL), BF16),
            pltpu.VMEM((3, 3, C, 3 * CL), BF16),
            pltpu.VMEM((3, 9 * CL, C), BF16),
            pltpu.VMEM((2, CL, 2 * W), F32),
            dma((3,)), dma((2,)),
            dma((2, 2)), dma((2, 2, 2)), dma((2,)),
            dma((2,)), dma((2, Z - 1)),
            dma((1,)), dma((1,)), dma((1,)), dma((1,)),
            dma((4,)), dma((2,)), dma((2, 2)), dma((2, 2)),
            dma((2, Z)), dma((Z,)),
        ],
        compiler_params=pltpu.CompilerParams(
            collective_id=0, has_side_effects=True, vmem_limit_bytes=40 * 1024 * 1024
        ),
    )(*(pltpu.with_memory_space_constraint(v, pltpu.HBM) for v in (
        latents.reshape(CL * T, W),
        cache_one.reshape(CL * 2, W),
        cache_two.reshape(CL * 2, W),
        gain_one.reshape(1, CL),
        bias_one.reshape(1, CL),
        gain_two.reshape(1, CL),
        bias_two.reshape(1, CL),
        weight_one,
        weight_two.reshape(3, 9 * CL, C),
    )))
    return out.reshape(CL, T, 2, 2, W).transpose(0, 1, 3, 2, 4).reshape(CL, T, 2, 2 * W)


def solution(mesh):
    return jax.shard_map(
        body,
        mesh=mesh,
        in_specs=(
            P("chan", None, "rows", None),
            P("chan", None, "rows", None),
            P("chan", None, "rows", None),
            P("chan"),
            P("chan"),
            P(None, None, None, None, "chan"),
            P("chan"),
            P("chan"),
            P(None, None, None, "chan", None),
        ),
        out_specs=P("chan", None, "rows", None),
        check_vma=False,
    )
```
